32 devices in a mesh: groups: 2 (over y), seq: 4 (over z), section: 2 (over x), chan: 2 (over core).
Axes of the slice: x: 2, y: 2, z: 4, core: 2. Of those that a mesh axis runs over, the one named last changes fastest.
Arguments:
- inputs: bfloat16 [8, 512, 384], P('groups', 'seq', 'chan'), parts along dimension 0, may hold values from -6 to 6
- cotangent: bfloat16 [8, 512, 384], P('groups', 'seq', 'chan'), parts along dimension 0, may hold values from -6 to 6
- conv_w: bfloat16 [2, 3, 384, 192], P('section', None, 'chan'), may hold values from -0.25 to 0.25
- mix_w: bfloat16 [2, 384, 384], P('section', None, 'chan'), may hold values from -0.3125 to 0.3125
- layer_ids: int32 [2], P('section'), may hold values from 0 to 1048575
- drop_salt: int32 [1], replicated, may hold values from 0 to 1048575
- starts: int32 [8], P('groups'), parts along dimension 0, may hold values from 0 to 67108863
Outputs:
- layer_grads: bfloat16 [2, 8, 512, 384], P('section', 'groups', 'seq', 'chan'), parts along dimension 1
- grad_conv: float32 [4, 3, 384, 192], P(('groups', 'section'), None, 'chan'), parts along dimension 0
- grad_mix: float32 [4, 384, 384], P(('groups', 'section'), None, 'chan'), parts along dimension 0
The draws below stay inside these ranges and needn't reach their ends.
There are 2 independent parts, one for each index of `groups`. The reference program is written for one: setup_inputs(seed, part) draws one part's arguments, and reference() takes and returns one part's arrays. A program takes and returns all parts, laid end to end along the dimension named above; an argument that names none is the same for every part. Nothing has to cross between parts.
All inputs are finite; a program needn't handle non-finite values.
Results may differ from the reference program's by a relative error of at most 0.0064.
Values may be sent and summed in bfloat16 or wider, within the bound.
A program may use at most 64 MiB of HBM per device.

```python
import math
import jax
import jax.numpy as jnp

C = 384
GW = 192
MB = 4
GROUPS = 2
LAYERS = 2
LENGTH = 512


def with_ends(drawn, stream_key, least, high):
    longest = drawn.shape.index(max(drawn.shape))
    spots = []
    for shift in (0, 1):
        where = [jax.random.randint(jax.random.fold_in(stream_key, axis), (), 0, length) for axis, length in enumerate(drawn.shape)]
        where[longest] = (where[longest] + shift) % drawn.shape[longest]
        spots.append(tuple(where))
    return drawn.at[spots[0]].set(least).at[spots[1]].set(high)


def levels(rng, extent, pieces, low, high):
    level = 1.0
    for position, blocks in pieces:
        draws = jax.random.uniform(jax.random.fold_in(jax.random.fold_in(rng, 6), position), (blocks,), jnp.float32, low / len(pieces), high / len(pieces))
        level = level * jnp.repeat(jnp.exp(draws), extent[position] // blocks).reshape((-1,) + (1,) * (len(extent) - 1 - position))
    return level


def noise(stream_key, extent, spread, most, pieces=(), held_as=jnp.bfloat16):
    values = spread * jax.random.normal(stream_key, extent, jnp.float32)
    if pieces:
        values = values * levels(stream_key, extent, pieces, -0.22, 0.18)
    return jnp.clip(values, -most, most).astype(held_as)


def setup_inputs(seed: int = 0, part: int = 0) -> dict:
    key_of = jax.random.split(jax.random.key(seed), 8)
    part_splits = jax.random.split(jax.random.fold_in(key_of[7], part), 8)
    return {
        "inputs": noise(part_splits[0], (MB, LENGTH, C), 1.0, 6.0, ((1, 4), (2, 2))),
        "cotangent": noise(part_splits[1], (MB, LENGTH, C), 1.0, 6.0, ((1, 4), (2, 2))),
        "conv_w": noise(key_of[2], (LAYERS, 3, C, GW), (3 * GW) ** -0.5, 0.25, ((0, 2), (2, 2))),
        "mix_w": noise(key_of[3], (LAYERS, C, C), C ** -0.5, 0.3125, ((0, 2), (2, 2))),
        "layer_ids": jax.random.randint(key_of[4], (LAYERS,), 0, 1048576).astype(jnp.int32),
        "drop_salt": jax.random.randint(key_of[5], (1,), 0, 1048576).astype(jnp.int32),
        "starts": with_ends(jax.random.randint(part_splits[6], (MB,), 0, 67108864), jax.random.fold_in(part_splits[6], 1), 0, 67108863).astype(jnp.int32),
    }


A_CONST = 0.7978845608028654
B_CONST = 0.044715

def gelu_pair(values):
    tangent = jnp.tanh(A_CONST * (values + B_CONST * values * values * values))
    result = 0.5 * values * (1.0 + tangent)
    slope = 0.5 * (1.0 + tangent) + 0.5 * values * (1.0 - tangent * tangent) * A_CONST * (1.0 + 0.134145 * values * values)
    return (result, slope)

def keep_scale(positions, channels, layer_key, salt_key):
    mixed = positions * 73856093
    mixed = jnp.bitwise_xor(mixed, channels * 19349663)
    mixed = jnp.bitwise_xor(mixed, layer_key * 83492791)
    mixed = jnp.bitwise_xor(mixed, salt_key)
    mixed = jnp.bitwise_xor(mixed, jnp.right_shift(mixed, 15))
    mixed = mixed * 668265261
    mixed = jnp.bitwise_xor(mixed, jnp.right_shift(mixed, 13))
    kept = jnp.bitwise_and(mixed, 1023) >= 205
    return jnp.where(kept, jnp.float32(1.25), jnp.float32(0.0))

def shifted(field, offset):
    total = field.shape[1]
    zeros = jnp.zeros((field.shape[0], abs(offset), field.shape[2]), field.dtype)
    if offset > 0:
        return jnp.concatenate([field[:, offset:], zeros], axis=1)
    return jnp.concatenate([zeros, field[:, :total + offset]], axis=1)

def grouped(field):
    return field.astype(jnp.float32).reshape(MB, LENGTH, GROUPS, GW)

def reference(inputs, cotangent, conv_w, mix_w, layer_ids, drop_salt, starts):
    positions = starts[:, None, None] + jnp.arange(LENGTH, dtype=jnp.int32)[None, :, None]
    channels = jnp.arange(C, dtype=jnp.int32)
    saved = []
    active = inputs
    for layer in range(LAYERS):
        dilation = LENGTH // 2 // 2 ** (LAYERS - 1 - layer)
        active_f = active.astype(jnp.float32)
        gel = gelu_pair(active_f)[0].astype(jnp.bfloat16)
        tapped = (shifted(gel, -dilation), gel, shifted(gel, dilation))
        kernel = conv_w[layer].astype(jnp.float32).reshape(3, GROUPS, GW, GW)
        summed = jnp.zeros((MB, LENGTH, GROUPS, GW), jnp.float32)
        for tap_index in range(3):
            summed = summed + jnp.einsum('mlgi,gio->mlgo', grouped(tapped[tap_index]), kernel[tap_index])
        pre_act = summed.reshape(MB, LENGTH, C)
        scaling = keep_scale(positions, channels, layer_ids[layer], drop_salt[0])
        hidden = (gelu_pair(pre_act)[0] * scaling).astype(jnp.bfloat16)
        mixed = jnp.einsum('mlc,ce->mle', hidden.astype(jnp.float32), mix_w[layer].astype(jnp.float32))
        saved.append((active_f, tapped, pre_act, hidden, scaling))
        active = (active_f + mixed).astype(jnp.bfloat16)
    factor = 1.0 / math.sqrt(MB * LENGTH)
    back = cotangent
    layer_out = [None] * LAYERS
    conv_out = [None] * LAYERS
    mix_out = [None] * LAYERS
    for layer in reversed(range(LAYERS)):
        dilation = LENGTH // 2 // 2 ** (LAYERS - 1 - layer)
        active_f, tapped, pre_act, hidden, scaling = saved[layer]
        back_f = back.astype(jnp.float32)
        mixing = mix_w[layer].astype(jnp.float32)
        back_hidden = jnp.einsum('mle,ce->mlc', back_f, mixing)
        mix_out[layer] = jnp.einsum('mlc,mle->ce', hidden.astype(jnp.float32), back_f) * factor
        back_pre = (back_hidden * scaling * gelu_pair(pre_act)[1]).astype(jnp.bfloat16)
        back_groups = grouped(back_pre)
        kernel = conv_w[layer].astype(jnp.float32).reshape(3, GROUPS, GW, GW)
        conv_terms = []
        for tap_index in range(3):
            term = jnp.einsum('mlgi,mlgo->gio', grouped(tapped[tap_index]), back_groups)
            conv_terms.append(term.reshape(C, GW) * factor)
        conv_out[layer] = jnp.stack(conv_terms)
        back_taps = (shifted(back_pre, dilation), back_pre, shifted(back_pre, -dilation))
        back_gel = jnp.zeros((MB, LENGTH, GROUPS, GW), jnp.float32)
        for tap_index in range(3):
            back_gel = back_gel + jnp.einsum('mlgo,gio->mlgi', grouped(back_taps[tap_index]), kernel[tap_index])
        back_gel = back_gel.reshape(MB, LENGTH, C)
        back = (back_f + back_gel * gelu_pair(active_f)[1]).astype(jnp.bfloat16)
        layer_out[layer] = back
    return (jnp.stack(layer_out), jnp.stack(conv_out), jnp.stack(mix_out))
```

```python
import functools
import math

import jax
import jax.numpy as jnp
from jax import lax
from jax.experimental import pallas as pl
from jax.experimental.pallas import tpu as pltpu
from jax.sharding import PartitionSpec as P

A_CONST = 0.7978845608028654
B_CONST = 0.044715


def from_behind(block, axis, distance):
    devices = range(lax.axis_size(axis))
    route = [(i - distance, i) for i in devices if i - distance in devices]
    return lax.ppermute(block, axis, route)


def gelu_pair(values):
    tangent = jnp.tanh(A_CONST * (values + B_CONST * values * values * values))
    result = 0.5 * values * (1.0 + tangent)
    slope = 0.5 * (1.0 + tangent) + 0.5 * values * (1.0 - tangent * tangent) * A_CONST * (
        1.0 + 0.134145 * values * values
    )
    return (result, slope)


def keep_scale(positions, channels, layer_key, salt_key):
    mixed = positions * 73856093
    mixed = jnp.bitwise_xor(mixed, channels * 19349663)
    mixed = jnp.bitwise_xor(mixed, layer_key * 83492791)
    mixed = jnp.bitwise_xor(mixed, salt_key)
    mixed = jnp.bitwise_xor(mixed, jnp.right_shift(mixed, 15))
    mixed = mixed * 668265261
    mixed = jnp.bitwise_xor(mixed, jnp.right_shift(mixed, 13))
    kept = jnp.bitwise_and(mixed, 1023) >= 205
    return jnp.where(kept, jnp.float32(1.25), jnp.float32(0.0))


def take_slot(store, slot_index):
    return lax.dynamic_index_in_dim(store, slot_index, 0, keepdims=False)


def put_slot(store, value, slot_index, valid):
    kept_value = jnp.where(valid, value, take_slot(store, slot_index))
    return lax.dynamic_update_index_in_dim(store, kept_value, slot_index, 0)


def pass_on(value, step_size):
    return from_behind(value, "section", step_size)


def general(inputs, cotangent, conv_w, mix_w, layer_ids, drop_salt, starts):
    sections = lax.axis_size("section")
    section_index = lax.axis_index("section")
    seq_count = lax.axis_size("seq")
    seq_index = lax.axis_index("seq")
    micro, rows, width = inputs.shape
    full_width = mix_w.shape[1]
    group_w = conv_w.shape[3]
    per_device = width // group_w
    length = rows * seq_count
    hop_count = seq_count.bit_length() - 1
    dilation = jnp.right_shift(jnp.int32(length // 2), sections - 1 - section_index)
    far_count = dilation // rows
    near_count = dilation % rows
    kernel = conv_w[0].reshape(3, per_device, group_w, group_w)
    mixing = mix_w[0]
    channels = lax.axis_index("chan") * width + jnp.arange(width, dtype=jnp.int32)
    offsets = seq_index * rows + jnp.arange(rows, dtype=jnp.int32)
    layer_key = layer_ids[0]
    salt_key = drop_salt[0]
    ticks = micro + sections - 1

    def scale_of(slot_index):
        positions = (lax.dynamic_index_in_dim(starts, slot_index, 0, keepdims=False) + offsets)[
            :, None
        ]
        return keep_scale(positions, channels, layer_key, salt_key)

    def walk(field, direction):
        distant = field
        beside = field
        for bit_index in range(hop_count + 1):
            step_size = direction * (1 << bit_index) if bit_index < hop_count else direction
            moved = from_behind(distant, "seq", step_size)
            if bit_index < hop_count:
                taken = jnp.bitwise_and(jnp.right_shift(far_count, bit_index), 1) == 1
                distant = jnp.where(taken, moved, distant)
            else:
                beside = moved
        return (distant, beside)

    def taps(field):
        ahead, ahead_next = walk(field, -1)
        behind, behind_prev = walk(field, 1)
        after = lax.dynamic_slice_in_dim(
            jnp.concatenate([ahead, ahead_next], axis=0), near_count, rows, 0
        )
        before = lax.dynamic_slice_in_dim(
            jnp.concatenate([behind_prev, behind], axis=0), rows - near_count, rows, 0
        )
        return (before, after)

    def split_groups(field):
        return field.reshape(rows, per_device, group_w)

    def convolve(before, centre, after):
        summed = jnp.zeros((rows, per_device, group_w), jnp.float32)
        for tap_index, tapped in enumerate((before, centre, after)):
            summed = summed + jnp.einsum(
                "sgi,gio->sgo",
                split_groups(tapped),
                kernel[tap_index],
                preferred_element_type=jnp.float32,
            )
        return summed.reshape(rows, width)

    def mix_in(piece):
        summed = jnp.dot(piece, mixing, preferred_element_type=jnp.float32)
        return (summed, piece)

    store = {
        "inbox": jnp.zeros((rows, width), jnp.bfloat16),
        "active": jnp.zeros((micro, rows, width), jnp.bfloat16),
        "before": jnp.zeros((micro, rows, width), jnp.bfloat16),
        "after": jnp.zeros((micro, rows, width), jnp.bfloat16),
        "pre_act": jnp.zeros((micro, rows, width), jnp.float32),
        "hidden": jnp.zeros((micro, rows, full_width), jnp.bfloat16),
    }
    store["scaling"] = jnp.zeros((micro, rows, width), jnp.float32)

    def forward_tick(tick_index, carry):
        slot_raw = tick_index - section_index
        valid = (slot_raw >= 0) & (slot_raw < micro)
        slot_index = jnp.clip(slot_raw, 0, micro - 1)
        active = jnp.where(section_index == 0, take_slot(inputs, slot_index), carry["inbox"])
        active_f = active.astype(jnp.float32)
        gel = gelu_pair(active_f)[0].astype(jnp.bfloat16)
        before, after = taps(gel)
        pre_act = convolve(before, gel, after)
        scaling = scale_of(slot_index)
        hidden = (gelu_pair(pre_act)[0] * scaling).astype(jnp.bfloat16)
        mixed, held = mix_in(lax.all_gather(hidden, "chan", axis=1, tiled=True))
        output = (active_f + mixed).astype(jnp.bfloat16)
        updated = dict(carry)
        updated["active"] = put_slot(carry["active"], active, slot_index, valid)
        updated["before"] = put_slot(carry["before"], before, slot_index, valid)
        updated["after"] = put_slot(carry["after"], after, slot_index, valid)
        updated["pre_act"] = put_slot(carry["pre_act"], pre_act, slot_index, valid)
        updated["hidden"] = put_slot(carry["hidden"], held, slot_index, valid)
        updated["scaling"] = put_slot(carry["scaling"], scaling, slot_index, valid)
        updated["inbox"] = pass_on(output, 1)
        return updated

    saved = lax.fori_loop(0, ticks, forward_tick, store)

    def backward_tick(tick_index, carry):
        inbox, conv_acc, mix_acc, grads_out = carry
        slot_raw = tick_index - (sections - 1 - section_index)
        valid = (slot_raw >= 0) & (slot_raw < micro)
        slot_index = jnp.clip(slot_raw, 0, micro - 1)
        incoming = jnp.where(section_index == sections - 1, take_slot(cotangent, slot_index), inbox)
        incoming_f = incoming.astype(jnp.float32)
        partial_terms = lax.dot_general(
            incoming, mixing, (((1,), (1,)), ((), ())), preferred_element_type=jnp.float32
        )
        back_hidden = lax.psum_scatter(partial_terms, "chan", scatter_dimension=1, tiled=True)
        held = take_slot(saved["hidden"], slot_index)
        mix_term = lax.dot_general(
            held, incoming, (((0,), (0,)), ((), ())), preferred_element_type=jnp.float32
        )
        mix_acc = mix_acc + jnp.where(valid, mix_term, 0.0)
        scaling = take_slot(saved["scaling"], slot_index)
        pre_act = take_slot(saved["pre_act"], slot_index)
        back_pre = (back_hidden * scaling * gelu_pair(pre_act)[1]).astype(jnp.bfloat16)
        back_groups = split_groups(back_pre)
        active_f = take_slot(saved["active"], slot_index).astype(jnp.float32)
        gel_value, act_slope = gelu_pair(active_f)
        tapped_set = (
            take_slot(saved["before"], slot_index),
            gel_value.astype(jnp.bfloat16),
            take_slot(saved["after"], slot_index),
        )
        conv_terms = []
        for tap_index in range(3):
            term = jnp.einsum(
                "sgi,sgo->gio",
                split_groups(tapped_set[tap_index]),
                back_groups,
                preferred_element_type=jnp.float32,
            )
            conv_terms.append(term.reshape(width, group_w))
        conv_acc = conv_acc + jnp.where(valid, jnp.stack(conv_terms), 0.0)
        back_before, back_after = taps(back_pre)
        back_gel = jnp.zeros((rows, per_device, group_w), jnp.float32)
        for tap_index, tapped in enumerate((back_after, back_pre, back_before)):
            back_gel = back_gel + jnp.einsum(
                "sgo,gio->sgi",
                split_groups(tapped),
                kernel[tap_index],
                preferred_element_type=jnp.float32,
            )
        gradient = (incoming_f + back_gel.reshape(rows, width) * act_slope).astype(jnp.bfloat16)
        grads_out = put_slot(grads_out, gradient, slot_index, valid)
        return (pass_on(gradient, -1), conv_acc, mix_acc, grads_out)

    start_carry = (
        jnp.zeros((rows, width), jnp.bfloat16),
        jnp.zeros((3, width, group_w), jnp.float32),
        jnp.zeros((full_width, width), jnp.float32),
        jnp.zeros((micro, rows, width), jnp.bfloat16),
    )
    unused_inbox, conv_acc, mix_acc, grads_out = lax.fori_loop(0, ticks, backward_tick, start_carry)
    conv_total, mix_total = lax.psum((conv_acc, mix_acc), "seq")
    factor = 1.0 / math.sqrt(micro * length)
    return (grads_out[None], (conv_total * factor)[None], (mix_total * factor)[None])


MESH = pl.DeviceIdType.MESH
CHUNK_ROWS = 48
LAG = 4
VMEM_LIMIT = 32 * 1024 * 1024


def tower_kernel(
    shape_info, ids, salt, starts_in, x_in, cot_in, conv_in, mix_in, lg_out, grads_out,
    starts, x_held, cot_held, act, cot, wconv, wmix, keys, keep, gel, act_slope, pre_slope, hid, part, out_part, in_part,
    back, back_pre, grad_f, grad_tx, grad_near, grad_far, grad_all,
    local_sem, tx, key_rx, x_rx, c_rx, w_rx, v_rx, h_rx, p_rx, near_rx, far_rx, all_rx, o_rx,
):
    blocks, rows, width, factor = shape_info
    me = lax.axis_index("seq")
    section = lax.axis_index("section")
    chan = lax.axis_index("chan")
    other_section = 1 - section
    other_chan = 1 - chan
    slab = lax.axis_index("groups")
    other_slab = 1 - slab
    steps = range(1, blocks)
    peers = {j: lax.rem(me + j, blocks) for j in steps}
    strides = (blocks // 4, blocks // 2)
    pairs = range(0, blocks, 2)
    chunks, chunk_rows = grad_f.shape[0], grad_f.shape[1]
    pair = me + 1 - 2 * lax.rem(me, 2)
    across_middle = blocks - 1 - me
    edge = jnp.logical_or(me == 0, me == blocks - 1)
    half = jnp.bfloat16

    def send(source, target, rx, device):
        return pltpu.make_async_remote_copy(
            src_ref=source, dst_ref=target, send_sem=tx, recv_sem=rx,
            device_id=device, device_id_type=MESH,
        )

    def arrived(landed, rx):
        pltpu.make_async_copy(landed, landed, rx).wait()

    barrier = pltpu.get_barrier_semaphore()
    for j in steps:
        pl.semaphore_signal(barrier, inc=1, device_id={"seq": peers[j]}, device_id_type=MESH)
    pl.semaphore_signal(barrier, inc=1, device_id={"section": other_section}, device_id_type=MESH)
    pl.semaphore_signal(barrier, inc=1, device_id={"chan": other_chan}, device_id_type=MESH)
    pl.semaphore_signal(barrier, inc=1, device_id={"groups": other_slab}, device_id_type=MESH)

    starts_copy = pltpu.make_async_copy(starts_in, starts, local_sem.at[0])
    own_copies = [
        pltpu.make_async_copy(x_in, x_held, local_sem.at[1]),
        pltpu.make_async_copy(cot_in, cot_held, local_sem.at[1]),
        pltpu.make_async_copy(conv_in, wconv.at[section], local_sem.at[1]),
        pltpu.make_async_copy(mix_in, wmix.at[section], local_sem.at[1]),
    ]
    for copy in [starts_copy, *own_copies]:
        copy.start()
    keys[section] = jnp.full(
        keys.shape[1:], jnp.bitwise_xor(ids[0] * 83492791, salt[0]), jnp.int32
    )
    starts_copy.wait()

    def fill_keep(layer):
        channels = chan * width + lax.broadcasted_iota(jnp.int32, (width, rows), 0)
        column = channels * 19349663
        for b in range(blocks):
            spots = starts[me] + b * rows + lax.broadcasted_iota(jnp.int32, (1, rows), 1)
            mixed = jnp.bitwise_xor(spots * 73856093, keys[layer][0:1, :])
            mixed = jnp.bitwise_xor(mixed, column)
            mixed = jnp.bitwise_xor(mixed, jnp.right_shift(mixed, 15))
            mixed = mixed * 668265261
            mixed = jnp.bitwise_xor(mixed, jnp.right_shift(mixed, 13))
            kept = jnp.bitwise_and(mixed, 1023) >= 205
            keep[layer, b] = jnp.where(kept, jnp.float32(1.25), jnp.float32(0.0))

    fill_keep(section)
    for copy in own_copies:
        copy.wait()
    act[me] = x_held[me]
    cot[me] = cot_held[me]
    pl.semaphore_wait(barrier, blocks + 2)

    across = {"section": other_section}
    beside = {"groups": other_slab}
    key_copy = send(keys.at[section], keys.at[section], key_rx, across)
    share = pl.ds(pl.multiple_of(slab * (width // 2), width // 2), width // 2)
    pieces = [*[(wconv, k) for k in range(3)], (wmix, None)]

    def piece_of(n, layer):
        ref, tap = pieces[n]
        return ref.at[layer, share] if tap is None else ref.at[layer, tap, share]

    weight_copies = [
        send(piece_of(n, section), piece_of(n, section), w_rx.at[n], across) for n in range(4)
    ]
    shared_copies = [
        send(
            piece_of(n, other_section), piece_of(n, other_section), v_rx.at[n // 3], beside
        )
        for n in range(4)
    ]

    def hand_on(n):
        weight_copies[n].wait_recv()
        shared_copies[n].start()

    def conv_arrived():
        arrived(wconv.at[other_section, :, pl.ds(0, width // 2)], v_rx.at[0])

    def mix_arrived():
        arrived(wmix.at[other_section, pl.ds(0, width // 2)], v_rx.at[1])

    x_copies = [
        send(x_held.at[peers[j]], act.at[me], x_rx, {"seq": peers[j]}) for j in steps
    ]
    cot_copies = [
        send(cot_held.at[peers[j]], cot.at[me], c_rx, {"seq": peers[j]}) for j in steps
    ]
    first = [*x_copies, key_copy, *weight_copies]
    for copy in first:
        copy.start()

    def dot(left, right):
        return jnp.dot(left, right, preferred_element_type=jnp.float32)

    def dot_first(left, right):
        return lax.dot_general(
            left, right, (((0,), (0,)), ((), ())), preferred_element_type=jnp.float32
        )

    def dot_last(left, right):
        return lax.dot_general(
            left, right, (((1,), (1,)), ((), ())), preferred_element_type=jnp.float32
        )

    def join(pieces):
        return jnp.concatenate(list(pieces), axis=1)

    def wide(ref, layer, low=0, high=blocks):
        return join(ref[layer, b] for b in range(low, high))

    def block_of(value, b):
        return value[:, b * rows : (b + 1) * rows]

    def activate(layer, b, value_f):
        gel_b, slope = gelu_pair(value_f)
        gel[layer, b] = gel_b.astype(half)
        act_slope[layer, b] = slope

    def shifted_sum(centre, behind, ahead, stride, b):
        total = block_of(centre, b)
        if b - stride >= 0:
            total = total + block_of(behind, b - stride)
        if b + stride < blocks:
            total = total + block_of(ahead, b)
        return total

    def convolve(layer, after_block):
        stride = strides[layer]
        centre = dot_first(wconv[layer, 1], wide(gel, layer))
        behind = dot_first(wconv[layer, 0], wide(gel, layer, 0, blocks - stride))
        ahead = dot_first(wconv[layer, 2], wide(gel, layer, stride, blocks))
        for b in range(blocks):
            value, slope = gelu_pair(shifted_sum(centre, behind, ahead, stride, b))
            scale = keep[layer, b]
            hid[layer, chan, b] = (value * scale).astype(half)
            pre_slope[layer, b] = slope * scale
            after_block(b)

    def hidden_copy(layer, b):
        place = hid.at[layer, chan, pl.ds(b, 2)]
        return send(place, place, h_rx.at[layer], {"chan": other_chan})

    def hidden_arrived(layer):
        arrived(hid.at[layer, other_chan], h_rx.at[layer])

    def send_hidden(layer):
        def after_block(b):
            if b % 2:
                hidden_copy(layer, b - 1).start()

        return after_block

    def hidden_wide(layer):
        return jnp.concatenate(
            [join(hid[layer, side, b] for b in range(blocks)) for side in range(2)], axis=0
        )

    def part_copy(layer, b):
        return send(
            out_part.at[layer, other_chan, pl.ds(b, 2)], in_part.at[layer, pl.ds(b, 2)],
            p_rx.at[layer, b // 2], {"chan": other_chan},
        )

    def spread_back(layer, incoming):
        for low in pairs:
            total = dot_first(wmix[layer], join(incoming(b) for b in (low, low + 1)))
            for side in range(2):
                for b in (low, low + 1):
                    piece = block_of(total[side * width : (side + 1) * width], b - low)
                    part[layer, side, b] = piece
                    out_part[layer, side, b] = piece.astype(half)
            part_copy(layer, low).start()

    def take_back_pre(layer):
        for low in pairs:
            part_copy(layer, low).wait_recv()
            for b in (low, low + 1):
                total = part[layer, chan, b] + in_part[layer, b].astype(jnp.float32)
                back_pre[layer, b] = (total * pre_slope[layer, b]).astype(half)

    def finish_layer(layer, incoming):
        stride = strides[layer]
        centre = dot(wconv[layer, 1], wide(back_pre, layer))
        behind = dot(wconv[layer, 2], wide(back_pre, layer, 0, blocks - stride))
        ahead = dot(wconv[layer, 0], wide(back_pre, layer, stride, blocks))
        for b in range(blocks):
            total = shifted_sum(centre, behind, ahead, stride, b) * act_slope[layer, b]
            back[layer, b] = (incoming(b).astype(jnp.float32) + total).astype(half)

    def near_copy(n):
        return send(
            grad_tx.at[n], grad_near.at[n], near_rx.at[n], {"seq": pair}
        )

    def far_copy(n):
        return send(
            grad_tx.at[n], grad_far.at[n], far_rx.at[n], {"seq": across_middle}
        )

    def all_copy(n):
        return send(
            grad_all.at[n], grads_out.at[n], all_rx, {"seq": pair}
        )

    def keep_copy(n):
        return pltpu.make_async_copy(grad_all.at[n], grads_out.at[n], local_sem.at[2])

    per_width = width // chunk_rows

    def hand_in(value, low):
        count = value.shape[0] // chunk_rows
        value = value.reshape(count, chunk_rows, 2 * width)
        grad_f[low : low + count] = value

        @pl.when(edge)
        def _():
            grad_tx[low : low + count] = value.astype(half)
            for n in range(low, low + count):
                near_copy(n).start()

    def mix_grads(layer, incoming):
        hand_in(dot_last(join(incoming(b) for b in range(blocks)), hidden_wide(layer)), 0)

    def conv_grads(layer):
        stride = strides[layer]
        gap = jnp.zeros((width, stride * rows), half)
        field = wide(gel, layer)
        behind = join([wide(back_pre, layer, stride, blocks), gap])
        ahead = join([gap, wide(back_pre, layer, 0, blocks - stride)])
        hand_in(dot_last(field, jnp.concatenate([behind, ahead], axis=0)), per_width)
        centre = dot_last(field, wide(back_pre, layer))
        middle = width // 2
        hand_in(join([centre[:middle], centre[middle:]]), 2 * per_width)

    def out_copy(j):
        return send(
            back.at[section, peers[j]], lg_out.at[me], o_rx, {"seq": peers[j]}
        )

    def out_own():
        return pltpu.make_async_copy(back.at[section, me], lg_out.at[me], local_sem.at[3])

    def send_out():
        for j in steps:
            out_copy(j).start()
        out_own().start()

    def from_cot(b):
        return cot[b]

    def from_back(b):
        return back[1, b]

    hand_on(0)
    hand_on(1)
    for copy in cot_copies:
        copy.start()
    key_copy.wait_recv()
    fill_keep(other_section)
    hand_on(2)
    hand_on(3)

    arrived(act.at[pl.ds(0, blocks - 1)], x_rx)
    for b in range(blocks):
        activate(0, b, act[b].astype(jnp.float32))

    @pl.when(section == 1)
    def _():
        conv_arrived()

    convolve(0, send_hidden(0))

    @pl.when(section == 1)
    def _():
        arrived(cot.at[pl.ds(0, blocks - 1)], c_rx)
        spread_back(1, from_cot)
        mix_arrived()

    hidden_arrived(0)
    mixed = dot(wmix[0], hidden_wide(0))
    for b in range(blocks):
        value = (act[b].astype(jnp.float32) + block_of(mixed, b)).astype(half)
        activate(1, b, value.astype(jnp.float32))

    @pl.when(section == 0)
    def _():
        arrived(cot.at[pl.ds(0, blocks - 1)], c_rx)
        mix_arrived()
        spread_back(1, from_cot)
        conv_arrived()
        convolve(1, lambda b: None)

    @pl.when(section == 1)
    def _():
        convolve(1, send_hidden(1))

    take_back_pre(1)

    @pl.when(section == 1)
    def _():
        hidden_arrived(1)
        mix_grads(1, from_cot)
        conv_grads(1)
        finish_layer(1, from_cot)

    @pl.when(section == 0)
    def _():
        finish_layer(1, from_cot)
        spread_back(0, from_back)
        mix_grads(0, from_back)
        take_back_pre(0)
        conv_grads(0)
        finish_layer(0, from_back)

    send_out()

    @pl.when(jnp.logical_not(edge))
    def _():
        for n in range(chunks + LAG):
            if n < chunks:
                near_copy(n).wait_recv()
                grad_tx[n] = (grad_f[n] + grad_near[n].astype(jnp.float32)).astype(half)
                far_copy(n).start()
            if n >= LAG:
                far_copy(n - LAG).wait_recv()
                total = grad_tx[n - LAG].astype(jnp.float32)
                total = total + grad_far[n - LAG].astype(jnp.float32)
                grad_all[n - LAG] = (total * factor).astype(half)
                all_copy(n - LAG).start()
                keep_copy(n - LAG).start()

    @pl.when(edge)
    def _():
        arrived(grad_all, all_rx)

    arrived(lg_out.at[pl.ds(0, blocks - 1)], o_rx)
    out_own().wait()
    sent = [*first, *shared_copies, *cot_copies, *[out_copy(j) for j in steps]]
    sent += [hidden_copy(0, low) for low in pairs] + [part_copy(1, low) for low in pairs]
    for copy in sent:
        copy.wait_send()

    @pl.when(section == 1)
    def _():
        for low in pairs:
            hidden_copy(1, low).wait_send()

    @pl.when(section == 0)
    def _():
        for low in pairs:
            part_copy(0, low).wait_send()

    @pl.when(edge)
    def _():
        for n in range(chunks):
            near_copy(n).wait_send()

    @pl.when(jnp.logical_not(edge))
    def _():
        for n in range(chunks):
            far_copy(n).wait_send()
            all_copy(n).wait_send()
        for n in range(chunks):
            keep_copy(n).wait()


def hand_out(grads, sums, grads_out, conv_out, mix_out, wide_conv, wide_mix, sems):
    width = wide_conv.shape[1]
    per_width = width // sums.shape[1]
    middle = width // 2

    def gathered(low, count):
        value = sums[low : low + count].astype(jnp.float32)
        return value.reshape(count * sums.shape[1], 2 * width)

    given = pltpu.make_async_copy(grads, grads_out, sems.at[0])
    given.start()
    wide_mix[...] = gathered(0, per_width)
    mixed = pltpu.make_async_copy(wide_mix, mix_out, sems.at[1])
    mixed.start()
    sides = gathered(per_width, per_width)
    wide_conv[0] = sides[:, :width]
    wide_conv[2] = sides[:, width:]
    centre = gathered(2 * per_width, per_width // 2)
    wide_conv[1, :middle] = centre[:, :width]
    wide_conv[1, middle:] = centre[:, width:]
    convolved = pltpu.make_async_copy(wide_conv, conv_out, sems.at[2])
    convolved.start()
    given.wait()
    mixed.wait()
    convolved.wait()


def fused(inputs, cotangent, conv_w, mix_w, layer_ids, drop_salt, starts):
    micro, rows, width = inputs.shape
    blocks = lax.axis_size("seq")
    factor = 1.0 / math.sqrt(micro * rows * blocks)
    half = jnp.bfloat16
    full = jnp.float32
    dma = pltpu.SemaphoreType.DMA
    field = (blocks, width, rows)
    chunk_rows = CHUNK_ROWS
    chunks = 5 * width // 2 // chunk_rows
    sums = (chunks, chunk_rows, 2 * width)
    smem = pltpu.SMEM
    scratch = [
        smem(starts.shape, jnp.int32),
        pltpu.VMEM(field, half),
        pltpu.VMEM(field, half),
        pltpu.VMEM(field, half),
        pltpu.VMEM(field, half),
        pltpu.VMEM((2, 3, width, width), half),
        pltpu.VMEM((2, width, 2 * width), half),
        pltpu.VMEM((2, 8, rows), jnp.int32),
        pltpu.VMEM((2,) + field, full),
        pltpu.VMEM((2,) + field, half),
        pltpu.VMEM((2,) + field, full),
        pltpu.VMEM((2,) + field, full),
        pltpu.VMEM((2, 2) + field, half),
        pltpu.VMEM((2, 2) + field, full),
        pltpu.VMEM((2, 2) + field, half),
        pltpu.VMEM((2,) + field, half),
        pltpu.VMEM((2,) + field, half),
        pltpu.VMEM((2,) + field, half),
        pltpu.VMEM(sums, full),
        pltpu.VMEM(sums, half),
        pltpu.VMEM(sums, half),
        pltpu.VMEM(sums, half),
        pltpu.VMEM(sums, half),
        dma((4,)), dma, dma, dma, dma, dma((4,)), dma((2,)), dma((2,)), dma((2, blocks // 2)),
        dma((chunks,)), dma((chunks,)), dma, dma,
    ]
    hbm = pl.BlockSpec(memory_space=pltpu.HBM)
    anywhere = pl.BlockSpec(memory_space=pl.ANY)
    vmem = pl.BlockSpec(memory_space=pltpu.VMEM)
    given = (
        starts, jnp.swapaxes(inputs, 1, 2), jnp.swapaxes(cotangent, 1, 2),
        conv_w[0], jnp.swapaxes(mix_w[0], 0, 1),
    )
    parts = pl.pallas_call(
        functools.partial(tower_kernel, (blocks, rows, width, factor)),
        out_shape=(pltpu.VMEM(field, half), pltpu.VMEM(sums, half)),
        in_specs=[pl.BlockSpec(memory_space=smem)] * 2 + [hbm] * 5,
        out_specs=(anywhere,) * 2,
        scratch_shapes=scratch,
        compiler_params=pltpu.CompilerParams(
            collective_id=0, has_side_effects=True, vmem_limit_bytes=VMEM_LIMIT
        ),
        name="tower",
    )(layer_ids, drop_salt, *[pltpu.with_memory_space_constraint(one, pltpu.HBM) for one in given])
    parts = [pltpu.with_memory_space_constraint(one, pltpu.VMEM) for one in parts]
    conv_shape, mix_shape = (3, width, width), (width, 2 * width)
    grads, conv_total, mix_total = pl.pallas_call(
        hand_out,
        out_shape=(
            jax.ShapeDtypeStruct(field, half),
            jax.ShapeDtypeStruct(conv_shape, full),
            jax.ShapeDtypeStruct(mix_shape, full),
        ),
        in_specs=[vmem] * 2,
        out_specs=(hbm,) * 3,
        scratch_shapes=[pltpu.VMEM(conv_shape, full), pltpu.VMEM(mix_shape, full), dma((3,))],
        compiler_params=pltpu.CompilerParams(vmem_limit_bytes=8 * 1024 * 1024),
        name="hand_out",
    )(*parts)
    return (jnp.swapaxes(grads, 1, 2)[None], conv_total[None], jnp.swapaxes(mix_total, 0, 1)[None])


def local(inputs, cotangent, conv_w, mix_w, layer_ids, drop_salt, starts):
    blocks = lax.axis_size("seq")
    micro, rows, width = inputs.shape
    fits = (
        lax.axis_size("section") == 2
        and lax.axis_size("groups") == 2
        and lax.axis_size("chan") == 2
        and micro == 4
        and blocks == 4
        and rows % 128 == 0
        and conv_w.shape[3] == width
        and width % (2 * CHUNK_ROWS) == 0
    )
    chosen = fused if fits else general
    return chosen(inputs, cotangent, conv_w, mix_w, layer_ids, drop_salt, starts)


def solution(mesh):
    placed = (
        P("groups", "seq", "chan"),
        P("groups", "seq", "chan"),
        P("section", None, "chan", None),
        P("section", None, "chan"),
        P("section"),
        P(),
        P("groups"),
    )
    return jax.shard_map(
        local,
        mesh=mesh,
        in_specs=placed,
        out_specs=(
            P("section", "groups", "seq", "chan"),
            P(("groups", "section"), None, "chan", None),
            P(("groups", "section"), None, "chan"),
        ),
        check_vma=False,
    )
```

```python
import functools
import math

import jax
import jax.numpy as jnp
from jax import lax
from jax.experimental import pallas as pl
from jax.experimental.pallas import tpu as pltpu
from jax.sharding import PartitionSpec as P

A_CONST = 0.7978845608028654
B_CONST = 0.044715


def from_behind(block, axis, distance):
    devices = range(lax.axis_size(axis))
    route = [(i - distance, i) for i in devices if i - distance in devices]
    return lax.ppermute(block, axis, route)


def gelu_pair(values):
    tangent = jnp.tanh(A_CONST * (values + B_CONST * values * values * values))
    result = 0.5 * values * (1.0 + tangent)
    slope = 0.5 * (1.0 + tangent) + 0.5 * values * (1.0 - tangent * tangent) * A_CONST * (
        1.0 + 0.134145 * values * values
    )
    return (result, slope)


def keep_scale(positions, channels, layer_key, salt_key):
    mixed = positions * 73856093
    mixed = jnp.bitwise_xor(mixed, channels * 19349663)
    mixed = jnp.bitwise_xor(mixed, layer_key * 83492791)
    mixed = jnp.bitwise_xor(mixed, salt_key)
    mixed = jnp.bitwise_xor(mixed, jnp.right_shift(mixed, 15))
    mixed = mixed * 668265261
    mixed = jnp.bitwise_xor(mixed, jnp.right_shift(mixed, 13))
    kept = jnp.bitwise_and(mixed, 1023) >= 205
    return jnp.where(kept, jnp.float32(1.25), jnp.float32(0.0))


def take_slot(store, slot_index):
    return lax.dynamic_index_in_dim(store, slot_index, 0, keepdims=False)


def put_slot(store, value, slot_index, valid):
    kept_value = jnp.where(valid, value, take_slot(store, slot_index))
    return lax.dynamic_update_index_in_dim(store, kept_value, slot_index, 0)


def pass_on(value, step_size):
    return from_behind(value, "section", step_size)


def general(inputs, cotangent, conv_w, mix_w, layer_ids, drop_salt, starts):
    sections = lax.axis_size("section")
    section_index = lax.axis_index("section")
    seq_count = lax.axis_size("seq")
    seq_index = lax.axis_index("seq")
    micro, rows, width = inputs.shape
    full_width = mix_w.shape[1]
    group_w = conv_w.shape[3]
    per_device = width // group_w
    length = rows * seq_count
    hop_count = seq_count.bit_length() - 1
    dilation = jnp.right_shift(jnp.int32(length // 2), sections - 1 - section_index)
    far_count = dilation // rows
    near_count = dilation % rows
    kernel = conv_w[0].reshape(3, per_device, group_w, group_w)
    mixing = mix_w[0]
    channels = lax.axis_index("chan") * width + jnp.arange(width, dtype=jnp.int32)
    offsets = seq_index * rows + jnp.arange(rows, dtype=jnp.int32)
    layer_key = layer_ids[0]
    salt_key = drop_salt[0]
    ticks = micro + sections - 1

    def scale_of(slot_index):
        positions = (lax.dynamic_index_in_dim(starts, slot_index, 0, keepdims=False) + offsets)[
            :, None
        ]
        return keep_scale(positions, channels, layer_key, salt_key)

    def walk(field, direction):
        distant = field
        beside = field
        for bit_index in range(hop_count + 1):
            step_size = direction * (1 << bit_index) if bit_index < hop_count else direction
            moved = from_behind(distant, "seq", step_size)
            if bit_index < hop_count:
                taken = jnp.bitwise_and(jnp.right_shift(far_count, bit_index), 1) == 1
                distant = jnp.where(taken, moved, distant)
            else:
                beside = moved
        return (distant, beside)

    def taps(field):
        ahead, ahead_next = walk(field, -1)
        behind, behind_prev = walk(field, 1)
        after = lax.dynamic_slice_in_dim(
            jnp.concatenate([ahead, ahead_next], axis=0), near_count, rows, 0
        )
        before = lax.dynamic_slice_in_dim(
            jnp.concatenate([behind_prev, behind], axis=0), rows - near_count, rows, 0
        )
        return (before, after)

    def split_groups(field):
        return field.reshape(rows, per_device, group_w)

    def convolve(before, centre, after):
        summed = jnp.zeros((rows, per_device, group_w), jnp.float32)
        for tap_index, tapped in enumerate((before, centre, after)):
            summed = summed + jnp.einsum(
                "sgi,gio->sgo",
                split_groups(tapped),
                kernel[tap_index],
                preferred_element_type=jnp.float32,
            )
        return summed.reshape(rows, width)

    def mix_in(piece):
        summed = jnp.dot(piece, mixing, preferred_element_type=jnp.float32)
        return (summed, piece)

    store = {
        "inbox": jnp.zeros((rows, width), jnp.bfloat16),
        "active": jnp.zeros((micro, rows, width), jnp.bfloat16),
        "before": jnp.zeros((micro, rows, width), jnp.bfloat16),
        "after": jnp.zeros((micro, rows, width), jnp.bfloat16),
        "pre_act": jnp.zeros((micro, rows, width), jnp.float32),
        "hidden": jnp.zeros((micro, rows, full_width), jnp.bfloat16),
    }
    store["scaling"] = jnp.zeros((micro, rows, width), jnp.float32)

    def forward_tick(tick_index, carry):
        slot_raw = tick_index - section_index
        valid = (slot_raw >= 0) & (slot_raw < micro)
        slot_index = jnp.clip(slot_raw, 0, micro - 1)
        active = jnp.where(section_index == 0, take_slot(inputs, slot_index), carry["inbox"])
        active_f = active.astype(jnp.float32)
        gel = gelu_pair(active_f)[0].astype(jnp.bfloat16)
        before, after = taps(gel)
        pre_act = convolve(before, gel, after)
        scaling = scale_of(slot_index)
        hidden = (gelu_pair(pre_act)[0] * scaling).astype(jnp.bfloat16)
        mixed, held = mix_in(lax.all_gather(hidden, "chan", axis=1, tiled=True))
        output = (active_f + mixed).astype(jnp.bfloat16)
        updated = dict(carry)
        updated["active"] = put_slot(carry["active"], active, slot_index, valid)
        updated["before"] = put_slot(carry["before"], before, slot_index, valid)
        updated["after"] = put_slot(carry["after"], after, slot_index, valid)
        updated["pre_act"] = put_slot(carry["pre_act"], pre_act, slot_index, valid)
        updated["hidden"] = put_slot(carry["hidden"], held, slot_index, valid)
        updated["scaling"] = put_slot(carry["scaling"], scaling, slot_index, valid)
        updated["inbox"] = pass_on(output, 1)
        return updated

    saved = lax.fori_loop(0, ticks, forward_tick, store)

    def backward_tick(tick_index, carry):
        inbox, conv_acc, mix_acc, grads_out = carry
        slot_raw = tick_index - (sections - 1 - section_index)
        valid = (slot_raw >= 0) & (slot_raw < micro)
        slot_index = jnp.clip(slot_raw, 0, micro - 1)
        incoming = jnp.where(section_index == sections - 1, take_slot(cotangent, slot_index), inbox)
        incoming_f = incoming.astype(jnp.float32)
        partial_terms = lax.dot_general(
            incoming, mixing, (((1,), (1,)), ((), ())), preferred_element_type=jnp.float32
        )
        back_hidden = lax.psum_scatter(partial_terms, "chan", scatter_dimension=1, tiled=True)
        held = take_slot(saved["hidden"], slot_index)
        mix_term = lax.dot_general(
            held, incoming, (((0,), (0,)), ((), ())), preferred_element_type=jnp.float32
        )
        mix_acc = mix_acc + jnp.where(valid, mix_term, 0.0)
        scaling = take_slot(saved["scaling"], slot_index)
        pre_act = take_slot(saved["pre_act"], slot_index)
        back_pre = (back_hidden * scaling * gelu_pair(pre_act)[1]).astype(jnp.bfloat16)
        back_groups = split_groups(back_pre)
        active_f = take_slot(saved["active"], slot_index).astype(jnp.float32)
        gel_value, act_slope = gelu_pair(active_f)
        tapped_set = (
            take_slot(saved["before"], slot_index),
            gel_value.astype(jnp.bfloat16),
            take_slot(saved["after"], slot_index),
        )
        conv_terms = []
        for tap_index in range(3):
            term = jnp.einsum(
                "sgi,sgo->gio",
                split_groups(tapped_set[tap_index]),
                back_groups,
                preferred_element_type=jnp.float32,
            )
            conv_terms.append(term.reshape(width, group_w))
        conv_acc = conv_acc + jnp.where(valid, jnp.stack(conv_terms), 0.0)
        back_before, back_after = taps(back_pre)
        back_gel = jnp.zeros((rows, per_device, group_w), jnp.float32)
        for tap_index, tapped in enumerate((back_after, back_pre, back_before)):
            back_gel = back_gel + jnp.einsum(
                "sgo,gio->sgi",
                split_groups(tapped),
                kernel[tap_index],
                preferred_element_type=jnp.float32,
            )
        gradient = (incoming_f + back_gel.reshape(rows, width) * act_slope).astype(jnp.bfloat16)
        grads_out = put_slot(grads_out, gradient, slot_index, valid)
        return (pass_on(gradient, -1), conv_acc, mix_acc, grads_out)

    start_carry = (
        jnp.zeros((rows, width), jnp.bfloat16),
        jnp.zeros((3, width, group_w), jnp.float32),
        jnp.zeros((full_width, width), jnp.float32),
        jnp.zeros((micro, rows, width), jnp.bfloat16),
    )
    unused_inbox, conv_acc, mix_acc, grads_out = lax.fori_loop(0, ticks, backward_tick, start_carry)
    conv_total, mix_total = lax.psum((conv_acc, mix_acc), "seq")
    factor = 1.0 / math.sqrt(micro * length)
    return (grads_out[None], (conv_total * factor)[None], (mix_total * factor)[None])


MESH = pl.DeviceIdType.MESH
CHUNK_ROWS = 32
LAG = 7
VMEM_LIMIT = 32 * 1024 * 1024


def tower_kernel(
    shape_info, ids, salt, starts_in, x_in, cot_in, conv_in, mix_in, lg_out, grads_out,
    starts, x_held, cot_held, act, cot, wconv, wmix, keys, keep, gel, act_slope, pre_slope, hid, part, out_part, in_part,
    back, back_pre, grad_f, grad_tx, grad_near, grad_far, grad_all,
    local_sem, tx, key_rx, x_rx, c_rx, w_rx, v_rx, h_rx, p_rx, near_rx, far_rx, all_rx, o_rx,
):
    blocks, rows, width, factor = shape_info
    me = lax.axis_index("seq")
    section = lax.axis_index("section")
    chan = lax.axis_index("chan")
    other_section = 1 - section
    other_chan = 1 - chan
    slab = lax.axis_index("groups")
    other_slab = 1 - slab
    steps = range(1, blocks)
    peers = {j: lax.rem(me + j, blocks) for j in steps}
    strides = (blocks // 4, blocks // 2)
    pairs = range(0, blocks, 2)
    chunks, chunk_rows = grad_f.shape[0], grad_f.shape[1]
    pair = me + 1 - 2 * lax.rem(me, 2)
    across_middle = blocks - 1 - me
    edge = jnp.logical_or(me == 0, me == blocks - 1)
    half = jnp.bfloat16

    def send(source, target, rx, device):
        return pltpu.make_async_remote_copy(
            src_ref=source, dst_ref=target, send_sem=tx, recv_sem=rx,
            device_id=device, device_id_type=MESH,
        )

    def arrived(landed, rx):
        pltpu.make_async_copy(landed, landed, rx).wait()

    barrier = pltpu.get_barrier_semaphore()
    for j in steps:
        pl.semaphore_signal(barrier, inc=1, device_id={"seq": peers[j]}, device_id_type=MESH)
    pl.semaphore_signal(barrier, inc=1, device_id={"section": other_section}, device_id_type=MESH)
    pl.semaphore_signal(barrier, inc=1, device_id={"chan": other_chan}, device_id_type=MESH)
    pl.semaphore_signal(barrier, inc=1, device_id={"groups": other_slab}, device_id_type=MESH)

    starts_copy = pltpu.make_async_copy(starts_in, starts, local_sem.at[0])
    own_copies = [
        pltpu.make_async_copy(x_in, x_held, local_sem.at[1]),
        pltpu.make_async_copy(cot_in, cot_held, local_sem.at[1]),
        pltpu.make_async_copy(conv_in, wconv.at[section], local_sem.at[1]),
        pltpu.make_async_copy(mix_in, wmix.at[section], local_sem.at[1]),
    ]
    for copy in [starts_copy, *own_copies]:
        copy.start()
    keys[section] = jnp.full(
        keys.shape[1:], jnp.bitwise_xor(ids[0] * 83492791, salt[0]), jnp.int32
    )
    starts_copy.wait()

    def fill_keep(layer):
        channels = chan * width + lax.broadcasted_iota(jnp.int32, (width, rows), 0)
        column = channels * 19349663
        for b in range(blocks):
            spots = starts[me] + b * rows + lax.broadcasted_iota(jnp.int32, (1, rows), 1)
            mixed = jnp.bitwise_xor(spots * 73856093, keys[layer][0:1, :])
            mixed = jnp.bitwise_xor(mixed, column)
            mixed = jnp.bitwise_xor(mixed, jnp.right_shift(mixed, 15))
            mixed = mixed * 668265261
            mixed = jnp.bitwise_xor(mixed, jnp.right_shift(mixed, 13))
            kept = jnp.bitwise_and(mixed, 1023) >= 205
            keep[layer, b] = jnp.where(kept, jnp.float32(1.25), jnp.float32(0.0))

    fill_keep(section)
    for copy in own_copies:
        copy.wait()
    act[me] = x_held[me]
    cot[me] = cot_held[me]
    pl.semaphore_wait(barrier, blocks + 2)

    across = {"section": other_section}
    beside = {"groups": other_slab}
    key_copy = send(keys.at[section], keys.at[section], key_rx, across)
    share = pl.ds(pl.multiple_of(slab * (width // 2), width // 2), width // 2)
    weight_copies = [
        send(wconv.at[section, k, share], wconv.at[section, k, share], w_rx.at[k], across)
        for k in range(3)
    ]
    shared_copies = [
        send(
            wconv.at[other_section, k, share], wconv.at[other_section, k, share], v_rx, beside
        )
        for k in range(3)
    ]
    mix_copy = send(wmix.at[section], wmix.at[section], w_rx.at[3], across)

    def hand_on(k):
        weight_copies[k].wait_recv()
        shared_copies[k].start()

    def conv_arrived():
        arrived(wconv.at[other_section, :, pl.ds(0, width // 2)], v_rx)

    def mix_arrived():
        mix_copy.wait_recv()

    x_copies = [
        send(x_held.at[peers[j]], act.at[me], x_rx, {"seq": peers[j]}) for j in steps
    ]
    cot_copies = [
        send(cot_held.at[peers[j]], cot.at[me], c_rx, {"seq": peers[j]}) for j in steps
    ]
    first = [*x_copies, key_copy, *weight_copies]
    for copy in first:
        copy.start()

    def dot(left, right):
        return jnp.dot(left, right, preferred_element_type=jnp.float32)

    def dot_first(left, right):
        return lax.dot_general(
            left, right, (((0,), (0,)), ((), ())), preferred_element_type=jnp.float32
        )

    def dot_last(left, right):
        return lax.dot_general(
            left, right, (((1,), (1,)), ((), ())), preferred_element_type=jnp.float32
        )

    def join(pieces):
        return jnp.concatenate(list(pieces), axis=1)

    def wide(ref, layer, low=0, high=blocks):
        return join(ref[layer, b] for b in range(low, high))

    def block_of(value, b):
        return value[:, b * rows : (b + 1) * rows]

    def activate(layer, b, value_f):
        gel_b, slope = gelu_pair(value_f)
        gel[layer, b] = gel_b.astype(half)
        act_slope[layer, b] = slope

    def shifted_sum(centre, behind, ahead, stride, b):
        total = block_of(centre, b)
        if b - stride >= 0:
            total = total + block_of(behind, b - stride)
        if b + stride < blocks:
            total = total + block_of(ahead, b)
        return total

    def convolve(layer, after_block):
        stride = strides[layer]
        centre = dot_first(wconv[layer, 1], wide(gel, layer))
        behind = dot_first(wconv[layer, 0], wide(gel, layer, 0, blocks - stride))
        ahead = dot_first(wconv[layer, 2], wide(gel, layer, stride, blocks))
        for b in range(blocks):
            value, slope = gelu_pair(shifted_sum(centre, behind, ahead, stride, b))
            scale = keep[layer, b]
            hid[layer, chan, b] = (value * scale).astype(half)
            pre_slope[layer, b] = slope * scale
            after_block(b)

    def hidden_copy(layer, b):
        place = hid.at[layer, chan, pl.ds(b, 2)]
        return send(place, place, h_rx.at[layer], {"chan": other_chan})

    def hidden_arrived(layer):
        arrived(hid.at[layer, other_chan], h_rx.at[layer])

    def send_hidden(layer):
        def after_block(b):
            if b % 2:
                hidden_copy(layer, b - 1).start()

        return after_block

    def hidden_wide(layer):
        return jnp.concatenate(
            [join(hid[layer, side, b] for b in range(blocks)) for side in range(2)], axis=0
        )

    def part_copy(layer, b):
        return send(
            out_part.at[layer, other_chan, pl.ds(b, 2)], in_part.at[layer, pl.ds(b, 2)],
            p_rx.at[layer, b // 2], {"chan": other_chan},
        )

    def spread_back(layer, incoming):
        for low in pairs:
            total = dot_first(wmix[layer], join(incoming(b) for b in (low, low + 1)))
            for side in range(2):
                for b in (low, low + 1):
                    piece = block_of(total[side * width : (side + 1) * width], b - low)
                    part[layer, side, b] = piece
                    out_part[layer, side, b] = piece.astype(half)
            part_copy(layer, low).start()

    def take_back_pre(layer):
        for low in pairs:
            part_copy(layer, low).wait_recv()
            for b in (low, low + 1):
                total = part[layer, chan, b] + in_part[layer, b].astype(jnp.float32)
                back_pre[layer, b] = (total * pre_slope[layer, b]).astype(half)

    def finish_layer(layer, incoming):
        stride = strides[layer]
        centre = dot(wconv[layer, 1], wide(back_pre, layer))
        behind = dot(wconv[layer, 2], wide(back_pre, layer, 0, blocks - stride))
        ahead = dot(wconv[layer, 0], wide(back_pre, layer, stride, blocks))
        for b in range(blocks):
            total = shifted_sum(centre, behind, ahead, stride, b) * act_slope[layer, b]
            back[layer, b] = (incoming(b).astype(jnp.float32) + total).astype(half)

    def near_copy(n):
        return send(
            grad_tx.at[n], grad_near.at[n], near_rx.at[n], {"seq": pair}
        )

    def far_copy(n):
        return send(
            grad_tx.at[n], grad_far.at[n], far_rx.at[n], {"seq": across_middle}
        )

    def all_copy(n):
        return send(
            grad_all.at[n], grads_out.at[n], all_rx, {"seq": pair}
        )

    def keep_copy(n):
        return pltpu.make_async_copy(grad_all.at[n], grads_out.at[n], local_sem.at[2])

    per_width = width // chunk_rows
    offset = section * per_width

    def turn(n):
        return lax.rem(n + offset, chunks)

    def hand_in(value, low):
        count = value.shape[0] // chunk_rows
        value = value.reshape(count, chunk_rows, 2 * width)
        grad_f[low : low + count] = value

        @pl.when(edge)
        def _():
            grad_tx[low : low + count] = value.astype(half)
            for n in range(low, low + count):
                near_copy(n).start()

    def mix_grads(layer, incoming):
        hand_in(dot_last(join(incoming(b) for b in range(blocks)), hidden_wide(layer)), 0)

    def conv_grads(layer):
        stride = strides[layer]
        gap = jnp.zeros((width, stride * rows), half)
        field = wide(gel, layer)
        behind = join([wide(back_pre, layer, stride, blocks), gap])
        ahead = join([gap, wide(back_pre, layer, 0, blocks - stride)])
        hand_in(dot_last(field, jnp.concatenate([behind, ahead], axis=0)), per_width)
        centre = dot_last(field, wide(back_pre, layer))
        middle = width // 2
        hand_in(join([centre[:middle], centre[middle:]]), 2 * per_width)

    def out_copy(j):
        return send(
            back.at[section, peers[j]], lg_out.at[me], o_rx, {"seq": peers[j]}
        )

    def out_own():
        return pltpu.make_async_copy(back.at[section, me], lg_out.at[me], local_sem.at[3])

    def send_out():
        for j in steps:
            out_copy(j).start()
        out_own().start()

    def from_cot(b):
        return cot[b]

    def from_back(b):
        return back[1, b]

    hand_on(0)
    for copy in cot_copies:
        copy.start()
    mix_copy.start()
    hand_on(1)
    hand_on(2)
    key_copy.wait_recv()
    fill_keep(other_section)
    arrived(act.at[pl.ds(0, blocks - 1)], x_rx)
    for b in range(blocks):
        activate(0, b, act[b].astype(jnp.float32))

    @pl.when(section == 1)
    def _():
        conv_arrived()

    convolve(0, send_hidden(0))

    @pl.when(section == 1)
    def _():
        arrived(cot.at[pl.ds(0, blocks - 1)], c_rx)
        spread_back(1, from_cot)
        mix_arrived()

    hidden_arrived(0)
    mixed = dot(wmix[0], hidden_wide(0))
    for b in range(blocks):
        value = (act[b].astype(jnp.float32) + block_of(mixed, b)).astype(half)
        activate(1, b, value.astype(jnp.float32))

    @pl.when(section == 0)
    def _():
        arrived(cot.at[pl.ds(0, blocks - 1)], c_rx)
        mix_arrived()
        spread_back(1, from_cot)
        conv_arrived()
        convolve(1, lambda b: None)

    @pl.when(section == 1)
    def _():
        convolve(1, send_hidden(1))

    take_back_pre(1)

    @pl.when(section == 1)
    def _():
        conv_grads(1)
        hidden_arrived(1)
        mix_grads(1, from_cot)
        finish_layer(1, from_cot)

    @pl.when(section == 0)
    def _():
        finish_layer(1, from_cot)
        mix_grads(0, from_back)
        spread_back(0, from_back)
        take_back_pre(0)
        conv_grads(0)
        finish_layer(0, from_back)

    send_out()

    @pl.when(jnp.logical_not(edge))
    def _():
        for n in range(chunks + LAG):
            if n < chunks:
                t = turn(n)
                near_copy(t).wait_recv()
                grad_tx[t] = (grad_f[t] + grad_near[t].astype(jnp.float32)).astype(half)
                far_copy(t).start()
            if n >= LAG:
                t = turn(n - LAG)
                far_copy(t).wait_recv()
                total = grad_tx[t].astype(jnp.float32) + grad_far[t].astype(jnp.float32)
                grad_all[t] = (total * factor).astype(half)
                all_copy(t).start()
                keep_copy(t).start()

    @pl.when(edge)
    def _():
        arrived(grad_all, all_rx)

    arrived(lg_out.at[pl.ds(0, blocks - 1)], o_rx)
    out_own().wait()
    sent = [*first, mix_copy, *shared_copies, *cot_copies, *[out_copy(j) for j in steps]]
    sent += [hidden_copy(0, low) for low in pairs] + [part_copy(1, low) for low in pairs]
    for copy in sent:
        copy.wait_send()

    @pl.when(section == 1)
    def _():
        for low in pairs:
            hidden_copy(1, low).wait_send()

    @pl.when(section == 0)
    def _():
        for low in pairs:
            part_copy(0, low).wait_send()

    @pl.when(edge)
    def _():
        for n in range(chunks):
            near_copy(n).wait_send()

    @pl.when(jnp.logical_not(edge))
    def _():
        for n in range(chunks):
            far_copy(n).wait_send()
            all_copy(n).wait_send()
        for n in range(chunks):
            keep_copy(n).wait()


def hand_out(grads, sums, grads_out, conv_out, mix_out, wide_conv, wide_mix, sems):
    width = wide_conv.shape[1]
    per_width = width // sums.shape[1]
    middle = width // 2

    def gathered(low, count):
        value = sums[low : low + count].astype(jnp.float32)
        return value.reshape(count * sums.shape[1], 2 * width)

    given = pltpu.make_async_copy(grads, grads_out, sems.at[0])
    given.start()
    wide_mix[...] = gathered(0, per_width)
    mixed = pltpu.make_async_copy(wide_mix, mix_out, sems.at[1])
    mixed.start()
    sides = gathered(per_width, per_width)
    wide_conv[0] = sides[:, :width]
    wide_conv[2] = sides[:, width:]
    centre = gathered(2 * per_width, per_width // 2)
    wide_conv[1, :middle] = centre[:, :width]
    wide_conv[1, middle:] = centre[:, width:]
    convolved = pltpu.make_async_copy(wide_conv, conv_out, sems.at[2])
    convolved.start()
    given.wait()
    mixed.wait()
    convolved.wait()


def fused(inputs, cotangent, conv_w, mix_w, layer_ids, drop_salt, starts):
    micro, rows, width = inputs.shape
    blocks = lax.axis_size("seq")
    factor = 1.0 / math.sqrt(micro * rows * blocks)
    half = jnp.bfloat16
    full = jnp.float32
    dma = pltpu.SemaphoreType.DMA
    field = (blocks, width, rows)
    chunk_rows = CHUNK_ROWS
    chunks = 5 * width // 2 // chunk_rows
    sums = (chunks, chunk_rows, 2 * width)
    smem = pltpu.SMEM
    scratch = [
        smem(starts.shape, jnp.int32),
        pltpu.VMEM(field, half),
        pltpu.VMEM(field, half),
        pltpu.VMEM(field, half),
        pltpu.VMEM(field, half),
        pltpu.VMEM((2, 3, width, width), half),
        pltpu.VMEM((2, width, 2 * width), half),
        pltpu.VMEM((2, 8, rows), jnp.int32),
        pltpu.VMEM((2,) + field, full),
        pltpu.VMEM((2,) + field, half),
        pltpu.VMEM((2,) + field, full),
        pltpu.VMEM((2,) + field, full),
        pltpu.VMEM((2, 2) + field, half),
        pltpu.VMEM((2, 2) + field, full),
        pltpu.VMEM((2, 2) + field, half),
        pltpu.VMEM((2,) + field, half),
        pltpu.VMEM((2,) + field, half),
        pltpu.VMEM((2,) + field, half),
        pltpu.VMEM(sums, full),
        pltpu.VMEM(sums, half),
        pltpu.VMEM(sums, half),
        pltpu.VMEM(sums, half),
        pltpu.VMEM(sums, half),
        dma((4,)), dma, dma, dma, dma, dma((4,)), dma, dma((2,)), dma((2, blocks // 2)),
        dma((chunks,)), dma((chunks,)), dma, dma,
    ]
    hbm = pl.BlockSpec(memory_space=pltpu.HBM)
    anywhere = pl.BlockSpec(memory_space=pl.ANY)
    vmem = pl.BlockSpec(memory_space=pltpu.VMEM)
    given = (
        starts, jnp.swapaxes(inputs, 1, 2), jnp.swapaxes(cotangent, 1, 2),
        conv_w[0], jnp.swapaxes(mix_w[0], 0, 1),
    )
    parts = pl.pallas_call(
        functools.partial(tower_kernel, (blocks, rows, width, factor)),
        out_shape=(pltpu.VMEM(field, half), pltpu.VMEM(sums, half)),
        in_specs=[pl.BlockSpec(memory_space=smem)] * 2 + [hbm] * 5,
        out_specs=(anywhere,) * 2,
        scratch_shapes=scratch,
        compiler_params=pltpu.CompilerParams(
            collective_id=0, has_side_effects=True, vmem_limit_bytes=VMEM_LIMIT
        ),
        name="tower",
    )(layer_ids, drop_salt, *[pltpu.with_memory_space_constraint(one, pltpu.HBM) for one in given])
    parts = [pltpu.with_memory_space_constraint(one, pltpu.VMEM) for one in parts]
    conv_shape, mix_shape = (3, width, width), (width, 2 * width)
    grads, conv_total, mix_total = pl.pallas_call(
        hand_out,
        out_shape=(
            jax.ShapeDtypeStruct(field, half),
            jax.ShapeDtypeStruct(conv_shape, full),
            jax.ShapeDtypeStruct(mix_shape, full),
        ),
        in_specs=[vmem] * 2,
        out_specs=(hbm,) * 3,
        scratch_shapes=[pltpu.VMEM(conv_shape, full), pltpu.VMEM(mix_shape, full), dma((3,))],
        compiler_params=pltpu.CompilerParams(vmem_limit_bytes=8 * 1024 * 1024),
        name="hand_out",
    )(*parts)
    return (jnp.swapaxes(grads, 1, 2)[None], conv_total[None], jnp.swapaxes(mix_total, 0, 1)[None])


def local(inputs, cotangent, conv_w, mix_w, layer_ids, drop_salt, starts):
    blocks = lax.axis_size("seq")
    micro, rows, width = inputs.shape
    fits = (
        lax.axis_size("section") == 2
        and lax.axis_size("groups") == 2
        and lax.axis_size("chan") == 2
        and micro == 4
        and blocks == 4
        and rows % 128 == 0
        and conv_w.shape[3] == width
        and width % (2 * CHUNK_ROWS) == 0
    )
    chosen = fused if fits else general
    return chosen(inputs, cotangent, conv_w, mix_w, layer_ids, drop_salt, starts)


def solution(mesh):
    placed = (
        P("groups", "seq", "chan"),
        P("groups", "seq", "chan"),
        P("section", None, "chan", None),
        P("section", None, "chan"),
        P("section"),
        P(),
        P("groups"),
    )
    return jax.shard_map(
        local,
        mesh=mesh,
        in_specs=placed,
        out_specs=(
            P("section", "groups", "seq", "chan"),
            P(("groups", "section"), None, "chan", None),
            P(("groups", "section"), None, "chan"),
        ),
        check_vma=False,
    )
```

```python
import functools
import math

import jax
import jax.numpy as jnp
from jax import lax
from jax.experimental import pallas as pl
from jax.experimental.pallas import tpu as pltpu
from jax.sharding import PartitionSpec as P

A_CONST = 0.7978845608028654
B_CONST = 0.044715


def from_behind(block, axis, distance):
    devices = range(lax.axis_size(axis))
    route = [(i - distance, i) for i in devices if i - distance in devices]
    return lax.ppermute(block, axis, route)


def gelu_pair(values):
    tangent = jnp.tanh(A_CONST * (values + B_CONST * values * values * values))
    result = 0.5 * values * (1.0 + tangent)
    slope = 0.5 * (1.0 + tangent) + 0.5 * values * (1.0 - tangent * tangent) * A_CONST * (
        1.0 + 0.134145 * values * values
    )
    return (result, slope)


def keep_scale(positions, channels, layer_key, salt_key):
    mixed = positions * 73856093
    mixed = jnp.bitwise_xor(mixed, channels * 19349663)
    mixed = jnp.bitwise_xor(mixed, layer_key * 83492791)
    mixed = jnp.bitwise_xor(mixed, salt_key)
    mixed = jnp.bitwise_xor(mixed, jnp.right_shift(mixed, 15))
    mixed = mixed * 668265261
    mixed = jnp.bitwise_xor(mixed, jnp.right_shift(mixed, 13))
    kept = jnp.bitwise_and(mixed, 1023) >= 205
    return jnp.where(kept, jnp.float32(1.25), jnp.float32(0.0))


def take_slot(store, slot_index):
    return lax.dynamic_index_in_dim(store, slot_index, 0, keepdims=False)


def put_slot(store, value, slot_index, valid):
    kept_value = jnp.where(valid, value, take_slot(store, slot_index))
    return lax.dynamic_update_index_in_dim(store, kept_value, slot_index, 0)


def pass_on(value, step_size):
    return from_behind(value, "section", step_size)


def general(inputs, cotangent, conv_w, mix_w, layer_ids, drop_salt, starts):
    sections = lax.axis_size("section")
    section_index = lax.axis_index("section")
    seq_count = lax.axis_size("seq")
    seq_index = lax.axis_index("seq")
    micro, rows, width = inputs.shape
    full_width = mix_w.shape[1]
    group_w = conv_w.shape[3]
    per_device = width // group_w
    length = rows * seq_count
    hop_count = seq_count.bit_length() - 1
    dilation = jnp.right_shift(jnp.int32(length // 2), sections - 1 - section_index)
    far_count = dilation // rows
    near_count = dilation % rows
    kernel = conv_w[0].reshape(3, per_device, group_w, group_w)
    mixing = mix_w[0]
    channels = lax.axis_index("chan") * width + jnp.arange(width, dtype=jnp.int32)
    offsets = seq_index * rows + jnp.arange(rows, dtype=jnp.int32)
    layer_key = layer_ids[0]
    salt_key = drop_salt[0]
    ticks = micro + sections - 1

    def scale_of(slot_index):
        positions = (lax.dynamic_index_in_dim(starts, slot_index, 0, keepdims=False) + offsets)[
            :, None
        ]
        return keep_scale(positions, channels, layer_key, salt_key)

    def walk(field, direction):
        distant = field
        beside = field
        for bit_index in range(hop_count + 1):
            step_size = direction * (1 << bit_index) if bit_index < hop_count else direction
            moved = from_behind(distant, "seq", step_size)
            if bit_index < hop_count:
                taken = jnp.bitwise_and(jnp.right_shift(far_count, bit_index), 1) == 1
                distant = jnp.where(taken, moved, distant)
            else:
                beside = moved
        return (distant, beside)

    def taps(field):
        ahead, ahead_next = walk(field, -1)
        behind, behind_prev = walk(field, 1)
        after = lax.dynamic_slice_in_dim(
            jnp.concatenate([ahead, ahead_next], axis=0), near_count, rows, 0
        )
        before = lax.dynamic_slice_in_dim(
            jnp.concatenate([behind_prev, behind], axis=0), rows - near_count, rows, 0
        )
        return (before, after)

    def split_groups(field):
        return field.reshape(rows, per_device, group_w)

    def convolve(before, centre, after):
        summed = jnp.zeros((rows, per_device, group_w), jnp.float32)
        for tap_index, tapped in enumerate((before, centre, after)):
            summed = summed + jnp.einsum(
                "sgi,gio->sgo",
                split_groups(tapped),
                kernel[tap_index],
                preferred_element_type=jnp.float32,
            )
        return summed.reshape(rows, width)

    def mix_in(piece):
        summed = jnp.dot(piece, mixing, preferred_element_type=jnp.float32)
        return (summed, piece)

    store = {
        "inbox": jnp.zeros((rows, width), jnp.bfloat16),
        "active": jnp.zeros((micro, rows, width), jnp.bfloat16),
        "before": jnp.zeros((micro, rows, width), jnp.bfloat16),
        "after": jnp.zeros((micro, rows, width), jnp.bfloat16),
        "pre_act": jnp.zeros((micro, rows, width), jnp.float32),
        "hidden": jnp.zeros((micro, rows, full_width), jnp.bfloat16),
    }
    store["scaling"] = jnp.zeros((micro, rows, width), jnp.float32)

    def forward_tick(tick_index, carry):
        slot_raw = tick_index - section_index
        valid = (slot_raw >= 0) & (slot_raw < micro)
        slot_index = jnp.clip(slot_raw, 0, micro - 1)
        active = jnp.where(section_index == 0, take_slot(inputs, slot_index), carry["inbox"])
        active_f = active.astype(jnp.float32)
        gel = gelu_pair(active_f)[0].astype(jnp.bfloat16)
        before, after = taps(gel)
        pre_act = convolve(before, gel, after)
        scaling = scale_of(slot_index)
        hidden = (gelu_pair(pre_act)[0] * scaling).astype(jnp.bfloat16)
        mixed, held = mix_in(lax.all_gather(hidden, "chan", axis=1, tiled=True))
        output = (active_f + mixed).astype(jnp.bfloat16)
        updated = dict(carry)
        updated["active"] = put_slot(carry["active"], active, slot_index, valid)
        updated["before"] = put_slot(carry["before"], before, slot_index, valid)
        updated["after"] = put_slot(carry["after"], after, slot_index, valid)
        updated["pre_act"] = put_slot(carry["pre_act"], pre_act, slot_index, valid)
        updated["hidden"] = put_slot(carry["hidden"], held, slot_index, valid)
        updated["scaling"] = put_slot(carry["scaling"], scaling, slot_index, valid)
        updated["inbox"] = pass_on(output, 1)
        return updated

    saved = lax.fori_loop(0, ticks, forward_tick, store)

    def backward_tick(tick_index, carry):
        inbox, conv_acc, mix_acc, grads_out = carry
        slot_raw = tick_index - (sections - 1 - section_index)
        valid = (slot_raw >= 0) & (slot_raw < micro)
        slot_index = jnp.clip(slot_raw, 0, micro - 1)
        incoming = jnp.where(section_index == sections - 1, take_slot(cotangent, slot_index), inbox)
        incoming_f = incoming.astype(jnp.float32)
        partial_terms = lax.dot_general(
            incoming, mixing, (((1,), (1,)), ((), ())), preferred_element_type=jnp.float32
        )
        back_hidden = lax.psum_scatter(partial_terms, "chan", scatter_dimension=1, tiled=True)
        held = take_slot(saved["hidden"], slot_index)
        mix_term = lax.dot_general(
            held, incoming, (((0,), (0,)), ((), ())), preferred_element_type=jnp.float32
        )
        mix_acc = mix_acc + jnp.where(valid, mix_term, 0.0)
        scaling = take_slot(saved["scaling"], slot_index)
        pre_act = take_slot(saved["pre_act"], slot_index)
        back_pre = (back_hidden * scaling * gelu_pair(pre_act)[1]).astype(jnp.bfloat16)
        back_groups = split_groups(back_pre)
        active_f = take_slot(saved["active"], slot_index).astype(jnp.float32)
        gel_value, act_slope = gelu_pair(active_f)
        tapped_set = (
            take_slot(saved["before"], slot_index),
            gel_value.astype(jnp.bfloat16),
            take_slot(saved["after"], slot_index),
        )
        conv_terms = []
        for tap_index in range(3):
            term = jnp.einsum(
                "sgi,sgo->gio",
                split_groups(tapped_set[tap_index]),
                back_groups,
                preferred_element_type=jnp.float32,
            )
            conv_terms.append(term.reshape(width, group_w))
        conv_acc = conv_acc + jnp.where(valid, jnp.stack(conv_terms), 0.0)
        back_before, back_after = taps(back_pre)
        back_gel = jnp.zeros((rows, per_device, group_w), jnp.float32)
        for tap_index, tapped in enumerate((back_after, back_pre, back_before)):
            back_gel = back_gel + jnp.einsum(
                "sgo,gio->sgi",
                split_groups(tapped),
                kernel[tap_index],
                preferred_element_type=jnp.float32,
            )
        gradient = (incoming_f + back_gel.reshape(rows, width) * act_slope).astype(jnp.bfloat16)
        grads_out = put_slot(grads_out, gradient, slot_index, valid)
        return (pass_on(gradient, -1), conv_acc, mix_acc, grads_out)

    start_carry = (
        jnp.zeros((rows, width), jnp.bfloat16),
        jnp.zeros((3, width, group_w), jnp.float32),
        jnp.zeros((full_width, width), jnp.float32),
        jnp.zeros((micro, rows, width), jnp.bfloat16),
    )
    unused_inbox, conv_acc, mix_acc, grads_out = lax.fori_loop(0, ticks, backward_tick, start_carry)
    conv_total, mix_total = lax.psum((conv_acc, mix_acc), "seq")
    factor = 1.0 / math.sqrt(micro * length)
    return (grads_out[None], (conv_total * factor)[None], (mix_total * factor)[None])


MESH = pl.DeviceIdType.MESH
CHUNK_ROWS = 32
LAG = 7
VMEM_LIMIT = 32 * 1024 * 1024


def tower_kernel(
    shape_info, ids, salt, starts_in, x_in, cot_in, conv_in, mix_in, lg_out, grads_out,
    starts, x_held, cot_held, act, cot, wconv, wmix, keys, keep, gel, act_slope, pre_slope, hid, part, out_part, in_part,
    back, back_pre, grad_f, grad_tx, grad_near, grad_far, grad_all,
    local_sem, tx, near_tx, key_rx, x_rx, c_rx, w_rx, v_rx, h_rx, p_rx, near_rx, far_rx, all_rx, o_rx,
):
    blocks, rows, width, factor = shape_info
    me = lax.axis_index("seq")
    section = lax.axis_index("section")
    chan = lax.axis_index("chan")
    other_section = 1 - section
    other_chan = 1 - chan
    slab = lax.axis_index("groups")
    other_slab = 1 - slab
    steps = range(1, blocks)
    peers = {j: lax.rem(me + j, blocks) for j in steps}
    strides = (blocks // 4, blocks // 2)
    pairs = range(0, blocks, 2)
    chunks, chunk_rows = grad_f.shape[0], grad_f.shape[1]
    pair = me + 1 - 2 * lax.rem(me, 2)
    across_middle = blocks - 1 - me
    edge = jnp.logical_or(me == 0, me == blocks - 1)
    half = jnp.bfloat16

    def send(source, target, rx, device, tx=tx):
        return pltpu.make_async_remote_copy(
            src_ref=source, dst_ref=target, send_sem=tx, recv_sem=rx,
            device_id=device, device_id_type=MESH,
        )

    def arrived(landed, rx):
        pltpu.make_async_copy(landed, landed, rx).wait()

    barrier = pltpu.get_barrier_semaphore()
    for j in steps:
        pl.semaphore_signal(barrier, inc=1, device_id={"seq": peers[j]}, device_id_type=MESH)
    pl.semaphore_signal(barrier, inc=1, device_id={"section": other_section}, device_id_type=MESH)
    pl.semaphore_signal(barrier, inc=1, device_id={"chan": other_chan}, device_id_type=MESH)
    pl.semaphore_signal(barrier, inc=1, device_id={"groups": other_slab}, device_id_type=MESH)

    starts_copy = pltpu.make_async_copy(starts_in, starts, local_sem.at[0])
    own_copies = [
        pltpu.make_async_copy(x_in, x_held, local_sem.at[1]),
        pltpu.make_async_copy(cot_in, cot_held, local_sem.at[1]),
        pltpu.make_async_copy(conv_in, wconv.at[section], local_sem.at[1]),
        pltpu.make_async_copy(mix_in, wmix.at[section], local_sem.at[1]),
    ]
    for copy in [starts_copy, *own_copies]:
        copy.start()
    keys[section] = jnp.full(
        keys.shape[1:], jnp.bitwise_xor(ids[0] * 83492791, salt[0]), jnp.int32
    )
    starts_copy.wait()

    def fill_keep(layer):
        channels = chan * width + lax.broadcasted_iota(jnp.int32, (width, rows), 0)
        column = channels * 19349663
        for b in range(blocks):
            spots = starts[me] + b * rows + lax.broadcasted_iota(jnp.int32, (1, rows), 1)
            mixed = jnp.bitwise_xor(spots * 73856093, keys[layer][0:1, :])
            mixed = jnp.bitwise_xor(mixed, column)
            mixed = jnp.bitwise_xor(mixed, jnp.right_shift(mixed, 15))
            mixed = mixed * 668265261
            mixed = jnp.bitwise_xor(mixed, jnp.right_shift(mixed, 13))
            kept = jnp.bitwise_and(mixed, 1023) >= 205
            keep[layer, b] = jnp.where(kept, jnp.float32(1.25), jnp.float32(0.0))

    fill_keep(section)
    for copy in own_copies:
        copy.wait()
    act[me] = x_held[me]
    cot[me] = cot_held[me]
    pl.semaphore_wait(barrier, blocks + 2)

    across = {"section": other_section}
    beside = {"groups": other_slab}
    key_copy = send(keys.at[section], keys.at[section], key_rx, across)
    share = pl.ds(pl.multiple_of(slab * (width // 2), width // 2), width // 2)
    conv_copy = send(wconv.at[section], wconv.at[section], w_rx.at[0], across)
    mix_copy = send(wmix.at[section, share], wmix.at[section, share], w_rx.at[1], across)
    shared_copy = send(
        wmix.at[other_section, share], wmix.at[other_section, share], v_rx, beside
    )

    def conv_arrived():
        conv_copy.wait_recv()

    def mix_arrived():
        arrived(wmix.at[other_section, pl.ds(0, width // 2)], v_rx)

    x_copies = [
        send(x_held.at[peers[j]], act.at[me], x_rx, {"seq": peers[j]}) for j in steps
    ]
    cot_copies = [
        send(cot_held.at[peers[j]], cot.at[me], c_rx, {"seq": peers[j]}) for j in steps
    ]
    first = [mix_copy, *x_copies, key_copy, conv_copy]
    for copy in first:
        copy.start()

    def dot(left, right):
        return jnp.dot(left, right, preferred_element_type=jnp.float32)

    def dot_first(left, right):
        return lax.dot_general(
            left, right, (((0,), (0,)), ((), ())), preferred_element_type=jnp.float32
        )

    def dot_last(left, right):
        return lax.dot_general(
            left, right, (((1,), (1,)), ((), ())), preferred_element_type=jnp.float32
        )

    def join(pieces):
        return jnp.concatenate(list(pieces), axis=1)

    def wide(ref, layer, low=0, high=blocks):
        return join(ref[layer, b] for b in range(low, high))

    def block_of(value, b):
        return value[:, b * rows : (b + 1) * rows]

    def activate(layer, b, value_f):
        gel_b, slope = gelu_pair(value_f)
        gel[layer, b] = gel_b.astype(half)
        act_slope[layer, b] = slope

    def shifted_sum(centre, behind, ahead, stride, b):
        total = block_of(centre, b)
        if b - stride >= 0:
            total = total + block_of(behind, b - stride)
        if b + stride < blocks:
            total = total + block_of(ahead, b)
        return total

    def convolve(layer, after_block):
        stride = strides[layer]
        centre = dot_first(wconv[layer, 1], wide(gel, layer))
        behind = dot_first(wconv[layer, 0], wide(gel, layer, 0, blocks - stride))
        ahead = dot_first(wconv[layer, 2], wide(gel, layer, stride, blocks))
        for b in range(blocks):
            value, slope = gelu_pair(shifted_sum(centre, behind, ahead, stride, b))
            scale = keep[layer, b]
            hid[layer, chan, b] = (value * scale).astype(half)
            pre_slope[layer, b] = slope * scale
            after_block(b)

    def hidden_copy(layer, b):
        place = hid.at[layer, chan, pl.ds(b, 2)]
        return send(place, place, h_rx.at[layer], {"chan": other_chan})

    def hidden_arrived(layer):
        arrived(hid.at[layer, other_chan], h_rx.at[layer])

    def send_hidden(layer):
        def after_block(b):
            if b % 2:
                hidden_copy(layer, b - 1).start()

        return after_block

    def hidden_wide(layer):
        return jnp.concatenate(
            [join(hid[layer, side, b] for b in range(blocks)) for side in range(2)], axis=0
        )

    def part_copy(layer, b):
        return send(
            out_part.at[layer, other_chan, pl.ds(b, 2)], in_part.at[layer, pl.ds(b, 2)],
            p_rx.at[layer, b // 2], {"chan": other_chan},
        )

    def spread_back(layer, incoming):
        for low in pairs:
            total = dot_first(wmix[layer], join(incoming(b) for b in (low, low + 1)))
            for side in range(2):
                for b in (low, low + 1):
                    piece = block_of(total[side * width : (side + 1) * width], b - low)
                    part[layer, side, b] = piece
                    out_part[layer, side, b] = piece.astype(half)
            part_copy(layer, low).start()

    def take_back_pre(layer):
        for low in pairs:
            part_copy(layer, low).wait_recv()
            for b in (low, low + 1):
                total = part[layer, chan, b] + in_part[layer, b].astype(jnp.float32)
                back_pre[layer, b] = (total * pre_slope[layer, b]).astype(half)

    def finish_layer(layer, incoming):
        stride = strides[layer]
        centre = dot(wconv[layer, 1], wide(back_pre, layer))
        behind = dot(wconv[layer, 2], wide(back_pre, layer, 0, blocks - stride))
        ahead = dot(wconv[layer, 0], wide(back_pre, layer, stride, blocks))
        for b in range(blocks):
            total = shifted_sum(centre, behind, ahead, stride, b) * act_slope[layer, b]
            back[layer, b] = (incoming(b).astype(jnp.float32) + total).astype(half)

    def near_copy(n):
        return send(
            grad_tx.at[n], grad_near.at[n], near_rx.at[n], {"seq": pair}, near_tx
        )

    def far_copy(n):
        return send(
            grad_tx.at[n], grad_far.at[n], far_rx.at[n], {"seq": across_middle}
        )

    def all_copy(n):
        return send(
            grad_all.at[n], grads_out.at[n], all_rx, {"seq": pair}
        )

    def keep_copy(n):
        return pltpu.make_async_copy(grad_all.at[n], grads_out.at[n], local_sem.at[2])

    per_width = width // chunk_rows
    offset = section * per_width

    def turn(n):
        return lax.rem(n + offset, chunks)

    def hand_in(value, low):
        count = value.shape[0] // chunk_rows
        value = value.reshape(count, chunk_rows, 2 * width)
        grad_f[low : low + count] = value

        @pl.when(edge)
        def _():
            grad_tx[low : low + count] = value.astype(half)
            for n in range(low, low + count):
                near_copy(n).start()

    def mix_grads(layer, incoming):
        hand_in(dot_last(join(incoming(b) for b in range(blocks)), hidden_wide(layer)), 0)

    def conv_grads(layer):
        stride = strides[layer]
        gap = jnp.zeros((width, stride * rows), half)
        field = wide(gel, layer)
        behind = join([wide(back_pre, layer, stride, blocks), gap])
        ahead = join([gap, wide(back_pre, layer, 0, blocks - stride)])
        hand_in(dot_last(field, jnp.concatenate([behind, ahead], axis=0)), per_width)
        centre = dot_last(field, wide(back_pre, layer))
        middle = width // 2
        hand_in(join([centre[:middle], centre[middle:]]), 2 * per_width)

    side = me // (blocks // 2)
    soon, late = (pair, (blocks - 1) * (1 - side)), blocks // 2 - side

    def out_copy(peer):
        return send(back.at[section, peer], lg_out.at[me], o_rx, {"seq": peer})

    def out_own():
        return pltpu.make_async_copy(back.at[section, me], lg_out.at[me], local_sem.at[3])

    def send_out():
        for peer in soon:
            out_copy(peer).start()
        out_own().start()

    def from_cot(b):
        return cot[b]

    def from_back(b):
        return back[1, b]

    @pl.when(chan == 0)
    def _():
        for copy in cot_copies:
            copy.start()

    mix_copy.wait_recv()
    shared_copy.start()
    key_copy.wait_recv()
    fill_keep(other_section)
    arrived(act.at[pl.ds(0, blocks - 1)], x_rx)
    @pl.when(chan == 1)
    def _():
        for copy in cot_copies:
            copy.start()

    for b in range(blocks):
        activate(0, b, act[b].astype(jnp.float32))

    @pl.when(section == 1)
    def _():
        conv_arrived()

    convolve(0, send_hidden(0))

    @pl.when(section == 1)
    def _():
        arrived(cot.at[pl.ds(0, blocks - 1)], c_rx)
        spread_back(1, from_cot)
        mix_arrived()

    hidden_arrived(0)
    mixed = dot(wmix[0], hidden_wide(0))
    for b in range(blocks):
        value = (act[b].astype(jnp.float32) + block_of(mixed, b)).astype(half)
        activate(1, b, value.astype(jnp.float32))

    @pl.when(section == 0)
    def _():
        arrived(cot.at[pl.ds(0, blocks - 1)], c_rx)
        mix_arrived()
        spread_back(1, from_cot)
        conv_arrived()
        convolve(1, lambda b: None)

    @pl.when(section == 1)
    def _():
        convolve(1, send_hidden(1))

    take_back_pre(1)

    @pl.when(section == 1)
    def _():
        conv_grads(1)
        hidden_arrived(1)
        mix_grads(1, from_cot)
        finish_layer(1, from_cot)

    @pl.when(section == 0)
    def _():
        finish_layer(1, from_cot)
        mix_grads(0, from_back)
        spread_back(0, from_back)
        take_back_pre(0)
        conv_grads(0)
        finish_layer(0, from_back)

    send_out()

    @pl.when(jnp.logical_not(edge))
    def _():
        for n in range(chunks + LAG):
            if n == 0:
                out_copy(late).start()
            if n < chunks:
                t = turn(n)
                near_copy(t).wait_recv()
                grad_tx[t] = (grad_f[t] + grad_near[t].astype(jnp.float32)).astype(half)
                far_copy(t).start()
            if n >= LAG:
                t = turn(n - LAG)
                far_copy(t).wait_recv()
                total = grad_tx[t].astype(jnp.float32) + grad_far[t].astype(jnp.float32)
                grad_all[t] = (total * factor).astype(half)
                all_copy(t).start()
                keep_copy(t).start()

    @pl.when(edge)
    def _():
        for n in range(chunks):
            near_copy(n).wait_send()
        out_copy(late).start()
        arrived(grad_all, all_rx)

    arrived(lg_out.at[pl.ds(0, blocks - 1)], o_rx)
    out_own().wait()
    sent = [*first, shared_copy, *cot_copies, *[out_copy(peer) for peer in (*soon, late)]]
    sent += [hidden_copy(0, low) for low in pairs] + [part_copy(1, low) for low in pairs]
    for copy in sent:
        copy.wait_send()

    @pl.when(section == 1)
    def _():
        for low in pairs:
            hidden_copy(1, low).wait_send()

    @pl.when(section == 0)
    def _():
        for low in pairs:
            part_copy(0, low).wait_send()

    @pl.when(jnp.logical_not(edge))
    def _():
        for n in range(chunks):
            far_copy(n).wait_send()
            all_copy(n).wait_send()
        for n in range(chunks):
            keep_copy(n).wait()


def hand_out(grads, sums, grads_out, conv_out, mix_out, wide_conv, wide_mix, sem):
    width = wide_conv.shape[1]
    per_width = width // sums.shape[1]
    middle = width // 2

    def gathered(low, count):
        value = sums[low : low + count].astype(jnp.float32)
        return value.reshape(count * sums.shape[1], 2 * width)

    copies = [pltpu.make_async_copy(grads, grads_out, sem)]
    copies += [pltpu.make_async_copy(wide_conv.at[k], conv_out.at[k], sem) for k in range(3)]
    copies += [pltpu.make_async_copy(wide_mix, mix_out, sem)]
    copies[0].start()
    sides = gathered(per_width, per_width)
    wide_conv[0] = sides[:, :width]
    copies[1].start()
    wide_conv[2] = sides[:, width:]
    copies[3].start()
    centre = gathered(2 * per_width, per_width // 2)
    wide_conv[1, :middle] = centre[:, :width]
    wide_conv[1, middle:] = centre[:, width:]
    copies[2].start()
    wide_mix[...] = gathered(0, per_width)
    copies[4].start()
    for copy in copies:
        copy.wait()


def fused(inputs, cotangent, conv_w, mix_w, layer_ids, drop_salt, starts):
    micro, rows, width = inputs.shape
    blocks = lax.axis_size("seq")
    factor = 1.0 / math.sqrt(micro * rows * blocks)
    half = jnp.bfloat16
    full = jnp.float32
    dma = pltpu.SemaphoreType.DMA
    field = (blocks, width, rows)
    chunk_rows = CHUNK_ROWS
    chunks = 5 * width // 2 // chunk_rows
    sums = (chunks, chunk_rows, 2 * width)
    smem = pltpu.SMEM
    scratch = [
        smem(starts.shape, jnp.int32),
        pltpu.VMEM(field, half),
        pltpu.VMEM(field, half),
        pltpu.VMEM(field, half),
        pltpu.VMEM(field, half),
        pltpu.VMEM((2, 3, width, width), half),
        pltpu.VMEM((2, width, 2 * width), half),
        pltpu.VMEM((2, 8, rows), jnp.int32),
        pltpu.VMEM((2,) + field, full),
        pltpu.VMEM((2,) + field, half),
        pltpu.VMEM((2,) + field, full),
        pltpu.VMEM((2,) + field, full),
        pltpu.VMEM((2, 2) + field, half),
        pltpu.VMEM((2, 2) + field, full),
        pltpu.VMEM((2, 2) + field, half),
        pltpu.VMEM((2,) + field, half),
        pltpu.VMEM((2,) + field, half),
        pltpu.VMEM((2,) + field, half),
        pltpu.VMEM(sums, full),
        pltpu.VMEM(sums, half),
        pltpu.VMEM(sums, half),
        pltpu.VMEM(sums, half),
        pltpu.VMEM(sums, half),
        dma((4,)), dma, dma, dma, dma, dma, dma((2,)), dma, dma((2,)), dma((2, blocks // 2)),
        dma((chunks,)), dma((chunks,)), dma, dma,
    ]
    hbm = pl.BlockSpec(memory_space=pltpu.HBM)
    anywhere = pl.BlockSpec(memory_space=pl.ANY)
    vmem = pl.BlockSpec(memory_space=pltpu.VMEM)
    given = (
        starts, jnp.swapaxes(inputs, 1, 2), jnp.swapaxes(cotangent, 1, 2),
        conv_w[0], jnp.swapaxes(mix_w[0], 0, 1),
    )
    parts = pl.pallas_call(
        functools.partial(tower_kernel, (blocks, rows, width, factor)),
        out_shape=(pltpu.VMEM(field, half), pltpu.VMEM(sums, half)),
        in_specs=[pl.BlockSpec(memory_space=smem)] * 2 + [hbm] * 5,
        out_specs=(anywhere,) * 2,
        scratch_shapes=scratch,
        compiler_params=pltpu.CompilerParams(
            collective_id=0, has_side_effects=True, vmem_limit_bytes=VMEM_LIMIT
        ),
        name="tower",
    )(layer_ids, drop_salt, *[pltpu.with_memory_space_constraint(one, pltpu.HBM) for one in given])
    parts = [pltpu.with_memory_space_constraint(one, pltpu.VMEM) for one in parts]
    conv_shape, mix_shape = (3, width, width), (width, 2 * width)
    grads, conv_total, mix_total = pl.pallas_call(
        hand_out,
        out_shape=(
            jax.ShapeDtypeStruct(field, half),
            jax.ShapeDtypeStruct(conv_shape, full),
            jax.ShapeDtypeStruct(mix_shape, full),
        ),
        in_specs=[vmem] * 2,
        out_specs=(hbm,) * 3,
        scratch_shapes=[pltpu.VMEM(conv_shape, full), pltpu.VMEM(mix_shape, full), dma],
        compiler_params=pltpu.CompilerParams(vmem_limit_bytes=8 * 1024 * 1024),
        name="hand_out",
    )(*parts)
    return (jnp.swapaxes(grads, 1, 2)[None], conv_total[None], jnp.swapaxes(mix_total, 0, 1)[None])


def local(inputs, cotangent, conv_w, mix_w, layer_ids, drop_salt, starts):
    blocks = lax.axis_size("seq")
    micro, rows, width = inputs.shape
    fits = (
        lax.axis_size("section") == 2
        and lax.axis_size("groups") == 2
        and lax.axis_size("chan") == 2
        and micro == 4
        and blocks == 4
        and rows % 128 == 0
        and conv_w.shape[3] == width
        and width % (2 * CHUNK_ROWS) == 0
    )
    chosen = fused if fits else general
    return chosen(inputs, cotangent, conv_w, mix_w, layer_ids, drop_salt, starts)


def solution(mesh):
    placed = (
        P("groups", "seq", "chan"),
        P("groups", "seq", "chan"),
        P("section", None, "chan", None),
        P("section", None, "chan"),
        P("section"),
        P(),
        P("groups"),
    )
    return jax.shard_map(
        local,
        mesh=mesh,
        in_specs=placed,
        out_specs=(
            P("section", "groups", "seq", "chan"),
            P(("groups", "section"), None, "chan", None),
            P(("groups", "section"), None, "chan"),
        ),
        check_vma=False,
    )
```

```python
import functools
import math

import jax
import jax.numpy as jnp
from jax import lax
from jax.experimental import pallas as pl
from jax.experimental.pallas import tpu as pltpu
from jax.sharding import PartitionSpec as P

A_CONST = 0.7978845608028654
B_CONST = 0.044715


def from_behind(block, axis, distance):
    devices = range(lax.axis_size(axis))
    route = [(i - distance, i) for i in devices if i - distance in devices]
    return lax.ppermute(block, axis, route)


def gelu_pair(values):
    tangent = jnp.tanh(A_CONST * (values + B_CONST * values * values * values))
    result = 0.5 * values * (1.0 + tangent)
    slope = 0.5 * (1.0 + tangent) + 0.5 * values * (1.0 - tangent * tangent) * A_CONST * (
        1.0 + 0.134145 * values * values
    )
    return (result, slope)


def keep_scale(positions, channels, layer_key, salt_key):
    mixed = positions * 73856093
    mixed = jnp.bitwise_xor(mixed, channels * 19349663)
    mixed = jnp.bitwise_xor(mixed, layer_key * 83492791)
    mixed = jnp.bitwise_xor(mixed, salt_key)
    mixed = jnp.bitwise_xor(mixed, jnp.right_shift(mixed, 15))
    mixed = mixed * 668265261
    mixed = jnp.bitwise_xor(mixed, jnp.right_shift(mixed, 13))
    kept = jnp.bitwise_and(mixed, 1023) >= 205
    return jnp.where(kept, jnp.float32(1.25), jnp.float32(0.0))


def take_slot(store, slot_index):
    return lax.dynamic_index_in_dim(store, slot_index, 0, keepdims=False)


def put_slot(store, value, slot_index, valid):
    kept_value = jnp.where(valid, value, take_slot(store, slot_index))
    return lax.dynamic_update_index_in_dim(store, kept_value, slot_index, 0)


def pass_on(value, step_size):
    return from_behind(value, "section", step_size)


def general(inputs, cotangent, conv_w, mix_w, layer_ids, drop_salt, starts):
    sections = lax.axis_size("section")
    section_index = lax.axis_index("section")
    seq_count = lax.axis_size("seq")
    seq_index = lax.axis_index("seq")
    micro, rows, width = inputs.shape
    full_width = mix_w.shape[1]
    group_w = conv_w.shape[3]
    per_device = width // group_w
    length = rows * seq_count
    hop_count = seq_count.bit_length() - 1
    dilation = jnp.right_shift(jnp.int32(length // 2), sections - 1 - section_index)
    far_count = dilation // rows
    near_count = dilation % rows
    kernel = conv_w[0].reshape(3, per_device, group_w, group_w)
    mixing = mix_w[0]
    channels = lax.axis_index("chan") * width + jnp.arange(width, dtype=jnp.int32)
    offsets = seq_index * rows + jnp.arange(rows, dtype=jnp.int32)
    layer_key = layer_ids[0]
    salt_key = drop_salt[0]
    ticks = micro + sections - 1

    def scale_of(slot_index):
        positions = (lax.dynamic_index_in_dim(starts, slot_index, 0, keepdims=False) + offsets)[
            :, None
        ]
        return keep_scale(positions, channels, layer_key, salt_key)

    def walk(field, direction):
        distant = field
        beside = field
        for bit_index in range(hop_count + 1):
            step_size = direction * (1 << bit_index) if bit_index < hop_count else direction
            moved = from_behind(distant, "seq", step_size)
            if bit_index < hop_count:
                taken = jnp.bitwise_and(jnp.right_shift(far_count, bit_index), 1) == 1
                distant = jnp.where(taken, moved, distant)
            else:
                beside = moved
        return (distant, beside)

    def taps(field):
        ahead, ahead_next = walk(field, -1)
        behind, behind_prev = walk(field, 1)
        after = lax.dynamic_slice_in_dim(
            jnp.concatenate([ahead, ahead_next], axis=0), near_count, rows, 0
        )
        before = lax.dynamic_slice_in_dim(
            jnp.concatenate([behind_prev, behind], axis=0), rows - near_count, rows, 0
        )
        return (before, after)

    def split_groups(field):
        return field.reshape(rows, per_device, group_w)

    def convolve(before, centre, after):
        summed = jnp.zeros((rows, per_device, group_w), jnp.float32)
        for tap_index, tapped in enumerate((before, centre, after)):
            summed = summed + jnp.einsum(
                "sgi,gio->sgo",
                split_groups(tapped),
                kernel[tap_index],
                preferred_element_type=jnp.float32,
            )
        return summed.reshape(rows, width)

    def mix_in(piece):
        summed = jnp.dot(piece, mixing, preferred_element_type=jnp.float32)
        return (summed, piece)

    store = {
        "inbox": jnp.zeros((rows, width), jnp.bfloat16),
        "active": jnp.zeros((micro, rows, width), jnp.bfloat16),
        "before": jnp.zeros((micro, rows, width), jnp.bfloat16),
        "after": jnp.zeros((micro, rows, width), jnp.bfloat16),
        "pre_act": jnp.zeros((micro, rows, width), jnp.float32),
        "hidden": jnp.zeros((micro, rows, full_width), jnp.bfloat16),
    }
    store["scaling"] = jnp.zeros((micro, rows, width), jnp.float32)

    def forward_tick(tick_index, carry):
        slot_raw = tick_index - section_index
        valid = (slot_raw >= 0) & (slot_raw < micro)
        slot_index = jnp.clip(slot_raw, 0, micro - 1)
        active = jnp.where(section_index == 0, take_slot(inputs, slot_index), carry["inbox"])
        active_f = active.astype(jnp.float32)
        gel = gelu_pair(active_f)[0].astype(jnp.bfloat16)
        before, after = taps(gel)
        pre_act = convolve(before, gel, after)
        scaling = scale_of(slot_index)
        hidden = (gelu_pair(pre_act)[0] * scaling).astype(jnp.bfloat16)
        mixed, held = mix_in(lax.all_gather(hidden, "chan", axis=1, tiled=True))
        output = (active_f + mixed).astype(jnp.bfloat16)
        updated = dict(carry)
        updated["active"] = put_slot(carry["active"], active, slot_index, valid)
        updated["before"] = put_slot(carry["before"], before, slot_index, valid)
        updated["after"] = put_slot(carry["after"], after, slot_index, valid)
        updated["pre_act"] = put_slot(carry["pre_act"], pre_act, slot_index, valid)
        updated["hidden"] = put_slot(carry["hidden"], held, slot_index, valid)
        updated["scaling"] = put_slot(carry["scaling"], scaling, slot_index, valid)
        updated["inbox"] = pass_on(output, 1)
        return updated

    saved = lax.fori_loop(0, ticks, forward_tick, store)

    def backward_tick(tick_index, carry):
        inbox, conv_acc, mix_acc, grads_out = carry
        slot_raw = tick_index - (sections - 1 - section_index)
        valid = (slot_raw >= 0) & (slot_raw < micro)
        slot_index = jnp.clip(slot_raw, 0, micro - 1)
        incoming = jnp.where(section_index == sections - 1, take_slot(cotangent, slot_index), inbox)
        incoming_f = incoming.astype(jnp.float32)
        partial_terms = lax.dot_general(
            incoming, mixing, (((1,), (1,)), ((), ())), preferred_element_type=jnp.float32
        )
        back_hidden = lax.psum_scatter(partial_terms, "chan", scatter_dimension=1, tiled=True)
        held = take_slot(saved["hidden"], slot_index)
        mix_term = lax.dot_general(
            held, incoming, (((0,), (0,)), ((), ())), preferred_element_type=jnp.float32
        )
        mix_acc = mix_acc + jnp.where(valid, mix_term, 0.0)
        scaling = take_slot(saved["scaling"], slot_index)
        pre_act = take_slot(saved["pre_act"], slot_index)
        back_pre = (back_hidden * scaling * gelu_pair(pre_act)[1]).astype(jnp.bfloat16)
        back_groups = split_groups(back_pre)
        active_f = take_slot(saved["active"], slot_index).astype(jnp.float32)
        gel_value, act_slope = gelu_pair(active_f)
        tapped_set = (
            take_slot(saved["before"], slot_index),
            gel_value.astype(jnp.bfloat16),
            take_slot(saved["after"], slot_index),
        )
        conv_terms = []
        for tap_index in range(3):
            term = jnp.einsum(
                "sgi,sgo->gio",
                split_groups(tapped_set[tap_index]),
                back_groups,
                preferred_element_type=jnp.float32,
            )
            conv_terms.append(term.reshape(width, group_w))
        conv_acc = conv_acc + jnp.where(valid, jnp.stack(conv_terms), 0.0)
        back_before, back_after = taps(back_pre)
        back_gel = jnp.zeros((rows, per_device, group_w), jnp.float32)
        for tap_index, tapped in enumerate((back_after, back_pre, back_before)):
            back_gel = back_gel + jnp.einsum(
                "sgo,gio->sgi",
                split_groups(tapped),
                kernel[tap_index],
                preferred_element_type=jnp.float32,
            )
        gradient = (incoming_f + back_gel.reshape(rows, width) * act_slope).astype(jnp.bfloat16)
        grads_out = put_slot(grads_out, gradient, slot_index, valid)
        return (pass_on(gradient, -1), conv_acc, mix_acc, grads_out)

    start_carry = (
        jnp.zeros((rows, width), jnp.bfloat16),
        jnp.zeros((3, width, group_w), jnp.float32),
        jnp.zeros((full_width, width), jnp.float32),
        jnp.zeros((micro, rows, width), jnp.bfloat16),
    )
    unused_inbox, conv_acc, mix_acc, grads_out = lax.fori_loop(0, ticks, backward_tick, start_carry)
    conv_total, mix_total = lax.psum((conv_acc, mix_acc), "seq")
    factor = 1.0 / math.sqrt(micro * length)
    return (grads_out[None], (conv_total * factor)[None], (mix_total * factor)[None])


MESH = pl.DeviceIdType.MESH
CHUNK_ROWS = 32
LAG = 7
VMEM_LIMIT = 32 * 1024 * 1024


def tower_kernel(
    shape_info, ids, salt, starts_in, x_in, cot_in, conv_in, mix_in, lg_out, grads_out,
    starts, x_held, cot_held, act, cot, wconv, wmix, keys, keep, gel, act_slope, pre_slope, hid, part, out_part, in_part,
    back, back_pre, grad_f, grad_tx, grad_near, grad_far, grad_all,
    local_sem, tx, near_tx, key_rx, x_rx, c_rx, w_rx, v_rx, h_rx, p_rx, near_rx, far_rx, all_rx, o_rx,
):
    blocks, rows, width, factor = shape_info
    me = lax.axis_index("seq")
    section = lax.axis_index("section")
    chan = lax.axis_index("chan")
    other_section = 1 - section
    other_chan = 1 - chan
    slab = lax.axis_index("groups")
    other_slab = 1 - slab
    steps = range(1, blocks)
    peers = {j: lax.rem(me + j, blocks) for j in steps}
    start_first = [j - 1 + (j - 1 - me + blocks) // blocks for j in steps]
    strides = (blocks // 4, blocks // 2)
    pairs = range(0, blocks, 2)
    chunks, chunk_rows = grad_f.shape[0], grad_f.shape[1]
    pair = me + 1 - 2 * lax.rem(me, 2)
    across_middle = blocks - 1 - me
    edge = jnp.logical_or(me == 0, me == blocks - 1)
    half = jnp.bfloat16

    def send(source, target, rx, device, tx=tx):
        return pltpu.make_async_remote_copy(
            src_ref=source, dst_ref=target, send_sem=tx, recv_sem=rx,
            device_id=device, device_id_type=MESH,
        )

    def arrived(landed, rx):
        pltpu.make_async_copy(landed, landed, rx).wait()

    barrier = pltpu.get_barrier_semaphore()
    for j in steps:
        pl.semaphore_signal(barrier, inc=1, device_id={"seq": peers[j]}, device_id_type=MESH)
    pl.semaphore_signal(barrier, inc=1, device_id={"section": other_section}, device_id_type=MESH)
    pl.semaphore_signal(barrier, inc=1, device_id={"chan": other_chan}, device_id_type=MESH)
    pl.semaphore_signal(barrier, inc=1, device_id={"groups": other_slab}, device_id_type=MESH)

    starts_copy = pltpu.make_async_copy(starts_in, starts, local_sem.at[0])
    own_copies = [
        pltpu.make_async_copy(x_in, x_held, local_sem.at[1]),
        pltpu.make_async_copy(cot_in, cot_held, local_sem.at[1]),
        pltpu.make_async_copy(conv_in, wconv.at[section], local_sem.at[1]),
        pltpu.make_async_copy(mix_in, wmix.at[section], local_sem.at[1]),
    ]
    for copy in [starts_copy, *own_copies]:
        copy.start()
    keys[section] = jnp.full(
        keys.shape[1:], jnp.bitwise_xor(ids[0] * 83492791, salt[0]), jnp.int32
    )
    starts_copy.wait()

    def fill_keep(layer):
        channels = chan * width + lax.broadcasted_iota(jnp.int32, (width, rows), 0)
        column = channels * 19349663
        for b in range(blocks):
            spots = starts[me] + b * rows + lax.broadcasted_iota(jnp.int32, (1, rows), 1)
            mixed = jnp.bitwise_xor(spots * 73856093, keys[layer][0:1, :])
            mixed = jnp.bitwise_xor(mixed, column)
            mixed = jnp.bitwise_xor(mixed, jnp.right_shift(mixed, 15))
            mixed = mixed * 668265261
            mixed = jnp.bitwise_xor(mixed, jnp.right_shift(mixed, 13))
            kept = jnp.bitwise_and(mixed, 1023) >= 205
            keep[layer, b] = jnp.where(kept, jnp.float32(1.25), jnp.float32(0.0))

    fill_keep(section)
    for copy in own_copies:
        copy.wait()
    act[me] = x_held[me]
    cot[me] = cot_held[me]
    pl.semaphore_wait(barrier, blocks + 2)

    across = {"section": other_section}
    beside = {"groups": other_slab}
    key_copy = send(keys.at[section], keys.at[section], key_rx, across)
    share = pl.ds(pl.multiple_of(slab * (width // 2), width // 2), width // 2)
    conv_copy = send(wconv.at[section], wconv.at[section], w_rx.at[0], across)
    mix_copy = send(wmix.at[section, share], wmix.at[section, share], w_rx.at[1], across)
    shared_copy = send(
        wmix.at[other_section, share], wmix.at[other_section, share], v_rx, beside
    )

    def conv_arrived():
        conv_copy.wait_recv()

    def mix_arrived():
        arrived(wmix.at[other_section, pl.ds(0, width // 2)], v_rx)

    x_copies = [
        send(x_held.at[peer], act.at[me], x_rx, {"seq": peer}) for peer in start_first
    ]
    cot_copies = [
        send(cot_held.at[peer], cot.at[me], c_rx, {"seq": peer}) for peer in start_first
    ]
    first = [mix_copy, *x_copies, key_copy, conv_copy]
    for copy in first:
        copy.start()

    def dot(left, right):
        return jnp.dot(left, right, preferred_element_type=jnp.float32)

    def dot_first(left, right):
        return lax.dot_general(
            left, right, (((0,), (0,)), ((), ())), preferred_element_type=jnp.float32
        )

    def dot_last(left, right):
        return lax.dot_general(
            left, right, (((1,), (1,)), ((), ())), preferred_element_type=jnp.float32
        )

    def join(pieces):
        return jnp.concatenate(list(pieces), axis=1)

    def wide(ref, layer, low=0, high=blocks):
        return join(ref[layer, b] for b in range(low, high))

    def block_of(value, b):
        return value[:, b * rows : (b + 1) * rows]

    def activate(layer, b, value_f):
        gel_b, slope = gelu_pair(value_f)
        gel[layer, b] = gel_b.astype(half)
        act_slope[layer, b] = slope

    def shifted_sum(centre, behind, ahead, stride, b):
        total = block_of(centre, b)
        if b - stride >= 0:
            total = total + block_of(behind, b - stride)
        if b + stride < blocks:
            total = total + block_of(ahead, b)
        return total

    def convolve(layer, after_block):
        stride = strides[layer]
        centre = dot_first(wconv[layer, 1], wide(gel, layer))
        behind = dot_first(wconv[layer, 0], wide(gel, layer, 0, blocks - stride))
        ahead = dot_first(wconv[layer, 2], wide(gel, layer, stride, blocks))
        for b in range(blocks):
            value, slope = gelu_pair(shifted_sum(centre, behind, ahead, stride, b))
            scale = keep[layer, b]
            hid[layer, chan, b] = (value * scale).astype(half)
            pre_slope[layer, b] = slope * scale
            after_block(b)

    def hidden_copy(layer, b):
        place = hid.at[layer, chan, pl.ds(b, 2)]
        return send(place, place, h_rx.at[layer], {"chan": other_chan})

    def hidden_arrived(layer):
        arrived(hid.at[layer, other_chan], h_rx.at[layer])

    def send_hidden(layer):
        def after_block(b):
            if b % 2:
                hidden_copy(layer, b - 1).start()

        return after_block

    def hidden_wide(layer):
        return jnp.concatenate(
            [join(hid[layer, side, b] for b in range(blocks)) for side in range(2)], axis=0
        )

    def part_copy(layer, b):
        return send(
            out_part.at[layer, other_chan, pl.ds(b, 2)], in_part.at[layer, pl.ds(b, 2)],
            p_rx.at[layer, b // 2], {"chan": other_chan},
        )

    def spread_back(layer, incoming):
        for low in pairs:
            total = dot_first(wmix[layer], join(incoming(b) for b in (low, low + 1)))
            for side in range(2):
                for b in (low, low + 1):
                    piece = block_of(total[side * width : (side + 1) * width], b - low)
                    part[layer, side, b] = piece
                    out_part[layer, side, b] = piece.astype(half)
            part_copy(layer, low).start()

    def take_back_pre(layer):
        for low in pairs:
            part_copy(layer, low).wait_recv()
            for b in (low, low + 1):
                total = part[layer, chan, b] + in_part[layer, b].astype(jnp.float32)
                back_pre[layer, b] = (total * pre_slope[layer, b]).astype(half)

    def finish_layer(layer, incoming):
        stride = strides[layer]
        centre = dot(wconv[layer, 1], wide(back_pre, layer))
        behind = dot(wconv[layer, 2], wide(back_pre, layer, 0, blocks - stride))
        ahead = dot(wconv[layer, 0], wide(back_pre, layer, stride, blocks))
        for b in range(blocks):
            total = shifted_sum(centre, behind, ahead, stride, b) * act_slope[layer, b]
            back[layer, b] = (incoming(b).astype(jnp.float32) + total).astype(half)

    def near_copy(n):
        return send(
            grad_tx.at[n], grad_near.at[n], near_rx.at[n], {"seq": pair}, near_tx
        )

    def far_copy(n):
        return send(
            grad_tx.at[n], grad_far.at[n], far_rx.at[n], {"seq": across_middle}
        )

    def all_copy(n):
        return send(
            grad_all.at[n], grads_out.at[n], all_rx, {"seq": pair}
        )

    def keep_copy(n):
        return pltpu.make_async_copy(grad_all.at[n], grads_out.at[n], local_sem.at[2])

    per_width = width // chunk_rows
    offset = section * per_width

    def turn(n):
        return lax.rem(n + offset, chunks)

    def hand_in(value, low):
        count = value.shape[0] // chunk_rows
        value = value.reshape(count, chunk_rows, 2 * width)
        grad_f[low : low + count] = value

        @pl.when(edge)
        def _():
            grad_tx[low : low + count] = value.astype(half)
            for n in range(low, low + count):
                near_copy(n).start()

    def mix_grads(layer, incoming):
        hand_in(dot_last(join(incoming(b) for b in range(blocks)), hidden_wide(layer)), 0)

    def conv_grads(layer):
        stride = strides[layer]
        gap = jnp.zeros((width, stride * rows), half)
        field = wide(gel, layer)
        behind = join([wide(back_pre, layer, stride, blocks), gap])
        ahead = join([gap, wide(back_pre, layer, 0, blocks - stride)])
        hand_in(dot_last(field, jnp.concatenate([behind, ahead], axis=0)), per_width)
        centre = dot_last(field, wide(back_pre, layer))
        middle = width // 2
        hand_in(join([centre[:middle], centre[middle:]]), 2 * per_width)

    side = me // (blocks // 2)
    soon, late = (pair, (blocks - 1) * (1 - side)), blocks // 2 - side

    def out_copy(peer):
        return send(back.at[section, peer], lg_out.at[me], o_rx, {"seq": peer})

    def out_own():
        return pltpu.make_async_copy(back.at[section, me], lg_out.at[me], local_sem.at[3])

    def send_out():
        for peer in soon:
            out_copy(peer).start()
        out_own().start()

    def from_cot(b):
        return cot[b]

    def from_back(b):
        return back[1, b]

    @pl.when(chan == 0)
    def _():
        for copy in cot_copies:
            copy.start()

    mix_copy.wait_recv()
    shared_copy.start()
    @pl.when(section == 1)
    def _():
        key_copy.wait_recv()
        fill_keep(other_section)

    arrived(act.at[pl.ds(0, blocks - 1)], x_rx)
    @pl.when(chan == 1)
    def _():
        for copy in cot_copies:
            copy.start()

    for b in range(blocks):
        activate(0, b, act[b].astype(jnp.float32))

    @pl.when(section == 1)
    def _():
        conv_arrived()

    convolve(0, send_hidden(0))

    @pl.when(section == 0)
    def _():
        key_copy.wait_recv()
        fill_keep(other_section)


    @pl.when(section == 1)
    def _():
        arrived(cot.at[pl.ds(0, blocks - 1)], c_rx)
        spread_back(1, from_cot)
        mix_arrived()

    hidden_arrived(0)
    mixed = dot(wmix[0], hidden_wide(0))
    for b in range(blocks):
        value = (act[b].astype(jnp.float32) + block_of(mixed, b)).astype(half)
        activate(1, b, value.astype(jnp.float32))

    @pl.when(section == 0)
    def _():
        arrived(cot.at[pl.ds(0, blocks - 1)], c_rx)
        mix_arrived()
        spread_back(1, from_cot)
        conv_arrived()
        convolve(1, lambda b: None)

    @pl.when(section == 1)
    def _():
        convolve(1, send_hidden(1))

    take_back_pre(1)

    @pl.when(section == 1)
    def _():
        conv_grads(1)
        finish_layer(1, from_cot)
        send_out()
        hidden_arrived(1)
        mix_grads(1, from_cot)

    @pl.when(section == 0)
    def _():
        finish_layer(1, from_cot)
        mix_grads(0, from_back)
        spread_back(0, from_back)
        take_back_pre(0)
        conv_grads(0)
        finish_layer(0, from_back)

    @pl.when(section == 0)
    def _():
        send_out()

    @pl.when(jnp.logical_not(edge))
    def _():
        for n in range(chunks + LAG):
            if n == 0:
                out_copy(late).start()
            if n < chunks:
                t = turn(n)
                near_copy(t).wait_recv()
                grad_tx[t] = (grad_f[t] + grad_near[t].astype(jnp.float32)).astype(half)
                far_copy(t).start()
            if n >= LAG:
                t = turn(n - LAG)
                far_copy(t).wait_recv()
                total = grad_tx[t].astype(jnp.float32) + grad_far[t].astype(jnp.float32)
                grad_all[t] = (total * factor).astype(half)
                all_copy(t).start()
                keep_copy(t).start()

    @pl.when(edge)
    def _():
        for n in range(chunks):
            near_copy(n).wait_send()
        out_copy(late).start()
        arrived(grad_all, all_rx)

    arrived(lg_out.at[pl.ds(0, blocks - 1)], o_rx)
    out_own().wait()
    sent = [*first, shared_copy, *cot_copies, *[out_copy(peer) for peer in (*soon, late)]]
    sent += [hidden_copy(0, low) for low in pairs] + [part_copy(1, low) for low in pairs]
    for copy in sent:
        copy.wait_send()

    @pl.when(section == 1)
    def _():
        for low in pairs:
            hidden_copy(1, low).wait_send()

    @pl.when(section == 0)
    def _():
        for low in pairs:
            part_copy(0, low).wait_send()

    @pl.when(jnp.logical_not(edge))
    def _():
        for n in range(chunks):
            far_copy(n).wait_send()
            all_copy(n).wait_send()
        for n in range(chunks):
            keep_copy(n).wait()


def hand_out(grads, sums, grads_out, conv_out, mix_out, wide_conv, wide_mix, sem):
    width = wide_conv.shape[1]
    per_width = width // sums.shape[1]
    middle = width // 2

    def gathered(low, count):
        value = sums[low : low + count].astype(jnp.float32)
        return value.reshape(count * sums.shape[1], 2 * width)

    copies = [pltpu.make_async_copy(grads, grads_out, sem)]
    copies += [pltpu.make_async_copy(wide_conv.at[k], conv_out.at[k], sem) for k in range(3)]
    copies += [pltpu.make_async_copy(wide_mix, mix_out, sem)]
    copies[0].start()
    sides = gathered(per_width, per_width)
    wide_conv[0] = sides[:, :width]
    copies[1].start()
    wide_conv[2] = sides[:, width:]
    copies[3].start()
    centre = gathered(2 * per_width, per_width // 2)
    wide_conv[1, :middle] = centre[:, :width]
    wide_conv[1, middle:] = centre[:, width:]
    copies[2].start()
    wide_mix[...] = gathered(0, per_width)
    copies[4].start()
    for copy in copies:
        copy.wait()


def fused(inputs, cotangent, conv_w, mix_w, layer_ids, drop_salt, starts):
    micro, rows, width = inputs.shape
    blocks = lax.axis_size("seq")
    factor = 1.0 / math.sqrt(micro * rows * blocks)
    half = jnp.bfloat16
    full = jnp.float32
    dma = pltpu.SemaphoreType.DMA
    field = (blocks, width, rows)
    chunk_rows = CHUNK_ROWS
    chunks = 5 * width // 2 // chunk_rows
    sums = (chunks, chunk_rows, 2 * width)
    smem = pltpu.SMEM
    scratch = [
        smem(starts.shape, jnp.int32),
        pltpu.VMEM(field, half),
        pltpu.VMEM(field, half),
        pltpu.VMEM(field, half),
        pltpu.VMEM(field, half),
        pltpu.VMEM((2, 3, width, width), half),
        pltpu.VMEM((2, width, 2 * width), half),
        pltpu.VMEM((2, 8, rows), jnp.int32),
        pltpu.VMEM((2,) + field, full),
        pltpu.VMEM((2,) + field, half),
        pltpu.VMEM((2,) + field, full),
        pltpu.VMEM((2,) + field, full),
        pltpu.VMEM((2, 2) + field, half),
        pltpu.VMEM((2, 2) + field, full),
        pltpu.VMEM((2, 2) + field, half),
        pltpu.VMEM((2,) + field, half),
        pltpu.VMEM((2,) + field, half),
        pltpu.VMEM((2,) + field, half),
        pltpu.VMEM(sums, full),
        pltpu.VMEM(sums, half),
        pltpu.VMEM(sums, half),
        pltpu.VMEM(sums, half),
        pltpu.VMEM(sums, half),
        dma((4,)), dma, dma, dma, dma, dma, dma((2,)), dma, dma((2,)), dma((2, blocks // 2)),
        dma((chunks,)), dma((chunks,)), dma, dma,
    ]
    hbm = pl.BlockSpec(memory_space=pltpu.HBM)
    anywhere = pl.BlockSpec(memory_space=pl.ANY)
    vmem = pl.BlockSpec(memory_space=pltpu.VMEM)
    given = (
        starts, jnp.swapaxes(inputs, 1, 2), jnp.swapaxes(cotangent, 1, 2),
        conv_w[0], jnp.swapaxes(mix_w[0], 0, 1),
    )
    parts = pl.pallas_call(
        functools.partial(tower_kernel, (blocks, rows, width, factor)),
        out_shape=(pltpu.VMEM(field, half), pltpu.VMEM(sums, half)),
        in_specs=[pl.BlockSpec(memory_space=smem)] * 2 + [hbm] * 5,
        out_specs=(anywhere,) * 2,
        scratch_shapes=scratch,
        compiler_params=pltpu.CompilerParams(
            collective_id=0, has_side_effects=True, vmem_limit_bytes=VMEM_LIMIT
        ),
        name="tower",
    )(layer_ids, drop_salt, *[pltpu.with_memory_space_constraint(one, pltpu.HBM) for one in given])
    parts = [pltpu.with_memory_space_constraint(one, pltpu.VMEM) for one in parts]
    conv_shape, mix_shape = (3, width, width), (width, 2 * width)
    grads, conv_total, mix_total = pl.pallas_call(
        hand_out,
        out_shape=(
            jax.ShapeDtypeStruct(field, half),
            jax.ShapeDtypeStruct(conv_shape, full),
            jax.ShapeDtypeStruct(mix_shape, full),
        ),
        in_specs=[vmem] * 2,
        out_specs=(hbm,) * 3,
        scratch_shapes=[pltpu.VMEM(conv_shape, full), pltpu.VMEM(mix_shape, full), dma],
        compiler_params=pltpu.CompilerParams(vmem_limit_bytes=8 * 1024 * 1024),
        name="hand_out",
    )(*parts)
    return (jnp.swapaxes(grads, 1, 2)[None], conv_total[None], jnp.swapaxes(mix_total, 0, 1)[None])


def local(inputs, cotangent, conv_w, mix_w, layer_ids, drop_salt, starts):
    blocks = lax.axis_size("seq")
    micro, rows, width = inputs.shape
    fits = (
        lax.axis_size("section") == 2
        and lax.axis_size("groups") == 2
        and lax.axis_size("chan") == 2
        and micro == 4
        and blocks == 4
        and rows % 128 == 0
        and conv_w.shape[3] == width
        and width % (2 * CHUNK_ROWS) == 0
    )
    chosen = fused if fits else general
    return chosen(inputs, cotangent, conv_w, mix_w, layer_ids, drop_salt, starts)


def solution(mesh):
    placed = (
        P("groups", "seq", "chan"),
        P("groups", "seq", "chan"),
        P("section", None, "chan", None),
        P("section", None, "chan"),
        P("section"),
        P(),
        P("groups"),
    )
    return jax.shard_map(
        local,
        mesh=mesh,
        in_specs=placed,
        out_specs=(
            P("section", "groups", "seq", "chan"),
            P(("groups", "section"), None, "chan", None),
            P(("groups", "section"), None, "chan"),
        ),
        check_vma=False,
    )
```
